32 devices in a mesh: floor: 4 (over y, x), strip: 8 (over z, core).
Axes of the slice: x: 2, y: 2, z: 4, core: 2. Of those that a mesh axis runs over, the one named last changes fastest.
Arguments:
- density: float32 [4, 4, 512, 2048], P('floor', None, 'strip'), may hold values from 0.2 to 2
- value_field: float32 [4, 4, 512, 2048], P('floor', None, 'strip'), may hold values from -3 to 3
- row_kernel: bfloat16 [512, 512], P('strip'), may hold values from -0.25 to 0.25
- column_kernel: bfloat16 [2048, 2048], replicated, may hold values from -0.125 to 0.125
- type_weight: float32 [4], replicated, may hold values from 0.5 to 2
- crowd_cost: float32 [4], replicated, may hold values from 0.1 to 1
- exit_drain: float32 [4], replicated, may hold values from 0.05 to 0.5
- exit_type: int32 [4, 128], P('floor', 'strip'), may hold values from 0 to 7
- landing_map: int32 [4, 64, 4], P(None, 'strip'), may hold values from 0 to 63, as said below
Outputs:
- final_density: float32 [4, 4, 512, 2048], P('floor', None, 'strip')
- final_value: float32 [4, 4, 512, 2048], P('floor', None, 'strip')
The draws below stay inside these ranges and needn't reach their ends.
Inputs may be any that keep to these rules, and one draw needn't show every extreme that they name: Each row of landing_map[f] gives a landing's source tile and source face row on floor f and its target tile and target face row on floor f - 1, in the same strip; tiles lie below 16 and face rows below 64, counted within the strip. Every strip of a floor has 8 landings, with distinct sources and distinct targets. `exit_type`: A value below 4 makes the tile an exit target of that occupant type; larger values mark tiles with no target.
All inputs are finite; a program needn't handle non-finite values.
Results may differ from the reference program's by a relative error of at most 0.0026.
Values may be sent and summed in bfloat16 or wider, within the bound.
A program may use at most 128 MiB of HBM per device.

```python
import math
import jax
import jax.numpy as jnp
from jax import lax

COLS = 2048
TYPES = 4
ROWS_DEV = 64
SUBSTEPS = 4
TILES = 16
LANDINGS = 8
FLOORS = 4
FLOOR_ROWS = 512
N_STRIP = 8


def draw_landing_map(key, part):
    cells = TILES * ROWS_DEV
    blocks = FLOORS * N_STRIP
    keys = jax.random.split(key, 2 * blocks)

    def pick(one_key):
        return jax.random.permutation(one_key, cells - 1)[:LANDINGS]
    chosen = jax.vmap(pick)(keys).astype(jnp.int32)
    block_ids = jnp.arange(2 * blocks, dtype=jnp.int32)
    slot_ids = jnp.arange(LANDINGS, dtype=jnp.int32)
    forced = (block_ids[:, None] % blocks == 0) & (slot_ids[None, :] == LANDINGS - 1)
    chosen = jnp.where(forced, jnp.int32(cells - 1), chosen)
    chosen = chosen.reshape(2, FLOORS, N_STRIP * LANDINGS)
    tile_index = chosen // ROWS_DEV
    row_index = chosen % ROWS_DEV
    return jnp.stack([tile_index[0], row_index[0], tile_index[1], row_index[1]], axis=-1)


def set_ends(drawn, stream_key, least, largest):
    index_at = [jax.random.randint(jax.random.fold_in(stream_key, axis), (), 0, length) for axis, length in enumerate(drawn.shape)]
    widest = drawn.shape.index(max(drawn.shape))
    neighbour = index_at[:widest] + [(index_at[widest] + 1) % drawn.shape[widest]] + index_at[widest + 1:]
    return drawn.at[tuple(index_at)].set(least).at[tuple(neighbour)].set(largest)


def shard_levels(own_key, shape, pieces, low, top_value):
    loudness, own = 1.0, jax.random.fold_in(own_key, 6)
    for position, parts in pieces:
        heights = jnp.exp(jax.random.uniform(jax.random.fold_in(own, position), (parts,), jnp.float32, low / len(pieces), top_value / len(pieces)))
        loudness = loudness * jnp.repeat(heights, shape[position] // parts).reshape([-1 if axis == position else 1 for axis in range(len(shape))])
    return loudness


def noise(rng, dims, scale, most, cuts=(), kind=jnp.bfloat16):
    drawn = scale * jax.random.normal(rng, dims, jnp.float32)
    if cuts:
        drawn = drawn * shard_levels(rng, dims, cuts, -0.22, 0.18)
    return jnp.clip(drawn, -most, most).astype(kind)


def setup_inputs(seed: int = 0) -> dict:
    arg_keys = jax.random.split(jax.random.key(seed), 10)
    return {
        "density": jnp.clip(jnp.exp(math.log(2.0) - 2.3025851 * jax.random.uniform(arg_keys[0], (FLOORS, TYPES, FLOOR_ROWS, COLS), jnp.float32) ** shard_levels(arg_keys[0], (FLOORS, TYPES, FLOOR_ROWS, COLS), ((0, 4), (2, 8)), -0.2, 0.2)), 0.2, 2.0),
        "value_field": noise(arg_keys[1], (FLOORS, TYPES, FLOOR_ROWS, COLS), 0.5, 3.0, ((0, 4), (2, 8)), jnp.float32),
        "row_kernel": noise(arg_keys[2], (FLOOR_ROWS, FLOOR_ROWS), FLOOR_ROWS ** -0.5, 0.25, ((0, 8),)),
        "column_kernel": noise(arg_keys[3], (COLS, COLS), COLS ** -0.5, 0.125),
        "type_weight": jnp.clip(jnp.exp(jax.random.uniform(arg_keys[4], (TYPES,), jnp.float32, math.log(0.5), math.log(2.0))), 0.5, 2.0),
        "crowd_cost": jnp.clip(jnp.exp(jax.random.uniform(arg_keys[5], (TYPES,), jnp.float32, math.log(0.1), math.log(1.0))), 0.1, 1.0),
        "exit_drain": jnp.clip(jnp.exp(jax.random.uniform(arg_keys[6], (TYPES,), jnp.float32, math.log(0.05), math.log(0.5))), 0.05, 0.5),
        "exit_type": set_ends(jax.random.randint(arg_keys[7], (FLOORS, N_STRIP * TILES), 0, 2 * TYPES), jax.random.fold_in(arg_keys[7], 1), 0, (2 * TYPES) - 1).astype(jnp.int32),
        "landing_map": draw_landing_map(jax.random.fold_in(arg_keys[9], 71), 0),
    }


time_step = 0.2
viscosity = 1.0
exit_reward = 2.0
stair_rate = 0.5


def advance(padded, crowd_cost, exit_drain, potential, target):
    types = crowd_cost.shape[0]
    dens_pad = padded[:types]
    val_pad = padded[types:]
    dens_now = dens_pad[:, 1:-1, 1:-1]
    value_now = val_pad[:, 1:-1, 1:-1]
    dens_near = (dens_pad[:, 2:, 1:-1], dens_pad[:, :-2, 1:-1], dens_pad[:, 1:-1, 2:], dens_pad[:, 1:-1, :-2])
    val_near = (val_pad[:, 2:, 1:-1], val_pad[:, :-2, 1:-1], val_pad[:, 1:-1, 2:], val_pad[:, 1:-1, :-2])
    laplace_value = val_near[0] + val_near[1] + val_near[2] + val_near[3] - 4.0 * value_now
    laplace_dens = dens_near[0] + dens_near[1] + dens_near[2] + dens_near[3] - 4.0 * dens_now
    grad_rows = 0.5 * (val_near[0] - val_near[1])
    grad_cols = 0.5 * (val_near[2] - val_near[3])
    flux_sum = 0.5 * (dens_near[0] + dens_now) * (val_near[0] - value_now) - 0.5 * (dens_now + dens_near[1]) * (value_now - val_near[1])
    flux_sum = flux_sum + 0.5 * (dens_near[2] + dens_now) * (val_near[2] - value_now) - 0.5 * (dens_now + dens_near[3]) * (value_now - val_near[3])
    new_value = value_now + time_step * (viscosity * laplace_value - 0.5 * (grad_rows * grad_rows + grad_cols * grad_cols) + crowd_cost[:, None, None] * potential[None] - exit_reward * target)
    moved = dens_now + time_step * (viscosity * laplace_dens + flux_sum)
    drained = moved * (1.0 - exit_drain[:, None, None] * target)
    return drained, new_value


def reference(density, value_field, row_kernel, column_kernel, type_weight, crowd_cost, exit_drain, exit_type, landing_map):
    tile_cols = COLS // TILES
    type_range = jnp.arange(TYPES, dtype=jnp.int32)
    tiles_all = exit_type.reshape(FLOORS, N_STRIP, TILES)
    target_small = (tiles_all[:, None, :, :] == type_range[None, :, None, None]).astype(jnp.float32)

    def floor_step(inputs):
        dens_now, value_now, small = inputs
        target = jnp.repeat(jnp.repeat(small, ROWS_DEV, axis=1), tile_cols, axis=2)
        crowd = jnp.sum(type_weight[:, None, None] * dens_now, axis=0).astype(jnp.bfloat16)
        mixed = jnp.dot(row_kernel, crowd, preferred_element_type=jnp.float32).astype(jnp.bfloat16)
        potential = jnp.dot(mixed, column_kernel, preferred_element_type=jnp.float32)
        stacked = jnp.concatenate([dens_now, value_now], axis=0)
        padded = jnp.pad(stacked, ((0, 0), (1, 1), (1, 1)), mode="edge")
        return advance(padded, crowd_cost, exit_drain, potential, target)

    strip_base = (jnp.arange(N_STRIP * LANDINGS, dtype=jnp.int32) // LANDINGS) * ROWS_DEV
    src_tile = landing_map[:, :, 0]
    src_row = landing_map[:, :, 1] + strip_base[None, :]
    dst_tile = landing_map[:, :, 2]
    dst_row = landing_map[:, :, 3] + strip_base[None, :]
    dst_tile_next = jnp.concatenate([dst_tile[1:], dst_tile[-1:]], axis=0)
    dst_row_next = jnp.concatenate([dst_row[1:], dst_row[-1:]], axis=0)

    def take_rows(view_floor, row_index, tile_index):
        return view_floor[:, row_index, tile_index, :]

    def place_rows(view_floor, row_src, tile_src, outflow, row_dst, tile_dst, incoming):
        view_floor = view_floor.at[:, row_src, tile_src, :].add(-outflow)
        return view_floor.at[:, row_dst, tile_dst, :].add(incoming)

    for substep in range(SUBSTEPS):
        drained, value_field = lax.map(floor_step, (density, value_field, target_small))
        view = drained.reshape(FLOORS, TYPES, FLOOR_ROWS, TILES, tile_cols)
        outflow = stair_rate * jax.vmap(take_rows)(view, src_row, src_tile)
        incoming = jnp.concatenate([outflow[1:], jnp.zeros_like(outflow[:1])], axis=0)
        view = jax.vmap(place_rows)(view, src_row, src_tile, outflow, dst_row_next, dst_tile_next, incoming)
        density = view.reshape(FLOORS, TYPES, FLOOR_ROWS, COLS)
    return density, value_field
```

```python
import functools

import jax
import jax.numpy as jnp
from jax import lax
from jax.experimental import pallas as pl
from jax.experimental.pallas import tpu as pltpu
from jax.sharding import PartitionSpec as P

SUBSTEPS = 4
TILES = 16
LANE = 128
TOP = 8

time_step = 0.2
viscosity = 1.0
exit_reward = 2.0
stair_rate = 0.5

MESH = pl.DeviceIdType.MESH


def kernel(
    strips, floors, landings, types, rows, width,
    dens_hbm, val_hbm, rk_hbm, ck_hbm, tw_hbm, cc_hbm, ed_hbm, et_hbm, lm_hbm,
    dens_out, val_out,
    m0, m1, u0, u1, ck, rk, crowd_send, crowd_recv, mix_send, mix_recv,
    hm_send, hm_recv, hu_send, hu_recv, out_send, out_recv,
    drain_fac, reward, keep_map, dst_map,
    tw_ref, cc_ref, ed_ref, et_ref, lm_ref,
    load_m, load_u, load_sem, store_m, store_u, rk_ssem, rk_rsem, rf_ssem, rf_rsem,
    c_ssem, c_rsem, x_ssem, x_rsem, hm_ssem, hm_rsem, hu_ssem, hu_rsem, o_ssem, o_rsem,
):
    me = lax.axis_index("strip")
    floor = lax.axis_index("floor")
    tiles = width // LANE
    cw = width // strips
    per = cw // LANE
    groups = rows // 8
    dq = rk.shape[-1]
    inner = pl.ds(TOP, rows)
    M, U = (m0, m1), (u0, u1)

    barrier = pltpu.get_barrier_semaphore()
    for off in range(1, strips):
        pl.semaphore_signal(barrier, inc=1, device_id={"strip": lax.rem(me + off, strips)}, device_id_type=MESH)
    for off in range(1, floors):
        pl.semaphore_signal(barrier, inc=1, device_id={"floor": lax.rem(floor + off, floors)}, device_id_type=MESH)

    def field_copy(hbm, buf, sem, c):
        return pltpu.make_async_copy(hbm.at[0, :, :, pl.ds(c * LANE, LANE)], buf.at[:, c, inner, :], sem.at[c])

    for c in range(tiles):
        field_copy(dens_hbm, m0, load_m, c).start()
    my_piece = pl.ds(pl.multiple_of(floor * dq, LANE), dq)
    own_rk = pltpu.make_async_copy(rk_hbm.at[:, my_piece], rk.at[floor, me], load_sem.at[0])
    own_rk.start()
    small = [
        pltpu.make_async_copy(src, dst, load_sem.at[1 + i])
        for i, (src, dst) in enumerate(
            ((tw_hbm, tw_ref), (cc_hbm, cc_ref), (ed_hbm, ed_ref), (et_hbm, et_ref), (lm_hbm, lm_ref))
        )
    ]
    for copy in small:
        copy.start()
    for c in range(tiles):
        field_copy(val_hbm, u0, load_u, c).start()
    load_ck = pltpu.make_async_copy(ck_hbm, ck, load_sem.at[6])
    load_ck.start()

    pl.semaphore_wait(barrier, strips + floors - 2)

    def strip_copy(src, dst, ssem, rsem, off):
        return pltpu.make_async_remote_copy(
            src_ref=src, dst_ref=dst, send_sem=ssem.at[off], recv_sem=rsem.at[off],
            device_id={"strip": lax.rem(me + off, strips)}, device_id_type=MESH,
        )

    def spread(step):
        return (strips // 2 + (1 - 2 * (step % 2)) * ((step + 1) // 2)) % strips

    order = [spread(step) for step in range(strips - 1)]

    def to_all(src_of, dst_ref, ssem, rsem):
        for off in order:
            strip_copy(src_of(lax.rem(me + off, strips)), dst_ref.at[me], ssem, rsem, off).start()

    def from_all(src_of, dst_ref, ssem, rsem):
        for off in range(1, strips):
            src = lax.rem(me + strips - off, strips)
            strip_copy(src_of(lax.rem(me + off, strips)), dst_ref.at[src], ssem, rsem, off).wait()

    def rk_hop(off):
        return pltpu.make_async_remote_copy(
            src_ref=rk.at[floor], dst_ref=rk.at[floor], send_sem=rf_ssem.at[off], recv_sem=rf_rsem.at[off],
            device_id={"floor": lax.rem(floor + off, floors)}, device_id_type=MESH,
        )

    def rk_landed(off):
        came = lax.rem(floor + floors - off, floors)
        return pltpu.make_async_remote_copy(
            src_ref=rk.at[floor], dst_ref=rk.at[came], send_sem=rf_ssem.at[off], recv_sem=rf_rsem.at[off],
            device_id={"floor": lax.rem(floor + off, floors)}, device_id_type=MESH,
        )

    def rim_copy(send, recv, ssem, rsem, t, side):
        return pltpu.make_async_remote_copy(
            src_ref=send.at[t, side], dst_ref=recv.at[t, 1 - side],
            send_sem=ssem.at[t, side], recv_sem=rsem.at[t, 1 - side],
            device_id={"strip": me - 1 if side == 0 else me + 1}, device_id_type=MESH,
        )

    def send_rims(buf, send, recv, ssem, rsem, t):
        def pack(side):
            at = TOP if side == 0 else TOP + rows - 1
            for k in range(types):
                for c in range(tiles):
                    send[t, side, k, c:c + 1, :] = buf[k, c, at:at + 1, :]
            rim_copy(send, recv, ssem, rsem, t, side).start()

        pl.when(me > 0)(lambda: pack(0))
        pl.when(me < strips - 1)(lambda: pack(1))

    def take_rims(buf, send, recv, ssem, rsem, t):
        def own(side):
            at = TOP if side == 0 else TOP + rows - 1
            to = TOP - 1 if side == 0 else TOP + rows
            for k in range(types):
                for c in range(tiles):
                    buf[k, c, to:to + 1, :] = buf[k, c, at:at + 1, :]

        def got(side):
            rim_copy(send, recv, ssem, rsem, t, side).wait_send()
            pltpu.make_async_remote_copy(
                src_ref=send.at[t, side], dst_ref=recv.at[t, side],
                send_sem=ssem.at[t, side], recv_sem=rsem.at[t, side],
                device_id={"strip": me - 1 if side == 0 else me + 1}, device_id_type=MESH,
            ).wait_recv()
            to = TOP - 1 if side == 0 else TOP + rows
            for k in range(types):
                for c in range(tiles):
                    buf[k, c, to:to + 1, :] = recv[t, side, k, c:c + 1, :]

        pl.when(me > 0)(lambda: got(0))
        pl.when(me == 0)(lambda: own(0))
        pl.when(me < strips - 1)(lambda: got(1))
        pl.when(me == strips - 1)(lambda: own(1))

    def crowd_of(t, initial):
        buf = M[t % 2]

        @pl.loop(0, strips)
        def _(step):
            off = lax.rem(strips // 2 + (1 - 2 * lax.rem(step, 2)) * lax.div(step + 1, 2), strips)
            dst = lax.rem(me + off, strips)
            for q in range(per):
                c = dst * per + q
                total = None
                if not initial:
                    keep = keep_map[c]
                    ids = dst_map[c]
                    slot = jnp.maximum(ids, 0)
                    landed = ids >= 0
                for k in range(types):
                    v = buf[k, c, inner, :]
                    if not initial:
                        if landings == 8:
                            add = jnp.concatenate([
                                jnp.take_along_axis(out_recv[t - 1, k], slot[r:r + 8], axis=0, mode="promise_in_bounds")
                                for r in range(0, rows, 8)
                            ], axis=0)
                            add = jnp.where(landed, add, 0.0)
                        else:
                            add = jnp.zeros_like(v)
                            for l in range(landings):
                                add = jnp.where(ids == l, out_recv[t - 1, k, l:l + 1, :], add)
                        v = v * keep + add
                        buf[k, c, inner, :] = v
                    term = tw_ref[k] * v
                    total = term if total is None else total + term
                if t < SUBSTEPS:
                    crowd_send[t, dst, :, q * LANE:(q + 1) * LANE] = total.astype(jnp.bfloat16)
                else:
                    pltpu.make_async_copy(
                        buf.at[:, c, inner, :],
                        dens_out.at[0, :, :, pl.ds(pl.multiple_of(c * LANE, LANE), LANE)],
                        store_m.at[c],
                    ).start()
            if t < SUBSTEPS:
                @pl.when(off > 0)
                def _():
                    strip_copy(crowd_send.at[t, dst], crowd_recv.at[t, me], c_ssem.at[t], c_rsem.at[t], off).start()

        if t < SUBSTEPS:
            crowd_recv[t, me] = crowd_send[t, me]

    def mix(t):
        from_all(lambda d: crowd_send.at[t, d], crowd_recv.at[t], c_ssem.at[t], c_rsem.at[t])
        crowd = crowd_recv[t].reshape(strips * rows, cw)
        weights = jnp.concatenate([rk[q].reshape(strips * rows, dq) for q in range(floors)], axis=1)
        mixed = jnp.dot(weights, crowd, preferred_element_type=jnp.float32)
        mix_send[t] = mixed.astype(jnp.bfloat16).reshape(strips, rows, cw)
        to_all(lambda d: mix_send.at[t, d], mix_recv.at[t], x_ssem.at[t], x_rsem.at[t])
        mix_recv[t, me] = mix_send[t, me]

    def add_potential(t):
        buf = U[(t + 1) % 2]
        from_all(lambda d: mix_send.at[t, d], mix_recv.at[t], x_ssem.at[t], x_rsem.at[t])
        step = 2 * LANE

        @pl.loop(0, width // step)
        def _(n):
            start = pl.multiple_of(n * step, step)
            acc = None
            for s in range(strips):
                d = jnp.dot(mix_recv[t, s], ck[s * cw:(s + 1) * cw, pl.ds(start, step)], preferred_element_type=jnp.float32)
                acc = d if acc is None else acc + d
            for q in range(2):
                c = 2 * n + q
                part = acc[:, q * LANE:(q + 1) * LANE]
                for k in range(types):
                    buf[k, c, inner, :] = buf[k, c, inner, :] + (time_step * cc_ref[k]) * part
                if t == SUBSTEPS - 1:
                    pltpu.make_async_copy(
                        buf.at[:, c, inner, :],
                        val_out.at[0, :, :, pl.ds(pl.multiple_of(c * LANE, LANE), LANE)],
                        store_u.at[c],
                    ).start()

    lane = lax.broadcasted_iota(jnp.int32, (8, LANE), 1)
    first, last = lane == 0, lane == LANE - 1

    def stencil(t, chunks):
        mb, ub, mo, uo = M[t % 2], U[t % 2], M[(t + 1) % 2], U[(t + 1) % 2]

        @pl.loop(0, types)
        def _(k):
            for r in chunks:
                lo = TOP + 8 * r
                here = slice(lo, lo + 8)
                m, u = mb[k, 0, here, :], ub[k, 0, here, :]
                m_from, u_from = m, u
                m_back, u_back = pltpu.roll(m, LANE - 1, 1), pltpu.roll(u, LANE - 1, 1)
                for c in range(tiles):
                    if c < tiles - 1:
                        m_next, u_next = mb[k, c + 1, here, :], ub[k, c + 1, here, :]
                        m_next_back, u_next_back = pltpu.roll(m_next, LANE - 1, 1), pltpu.roll(u_next, LANE - 1, 1)
                    else:
                        m_next, u_next, m_next_back, u_next_back = m, u, m, u
                    mr, ur = jnp.where(last, m_next_back, m_back), jnp.where(last, u_next_back, u_back)
                    m_on, u_on = pltpu.roll(m, 1, 1), pltpu.roll(u, 1, 1)
                    ml, ul = jnp.where(first, m_from, m_on), jnp.where(first, u_from, u_on)
                    mu, md = mb[k, c, lo - 1:lo + 7, :], mb[k, c, lo + 1:lo + 9, :]
                    uu, ud = ub[k, c, lo - 1:lo + 7, :], ub[k, c, lo + 1:lo + 9, :]
                    low = u - 2.0 * viscosity
                    flux = None
                    rise = None
                    for mn, un in ((mu, uu), (md, ud), (ml, ul), (mr, ur)):
                        p = un - low
                        flux = mn * p if flux is None else flux + mn * p
                        rise = p if rise is None else rise + p
                    gr = ud - uu
                    gc = ur - ul
                    stay = (1.0 - 8.0 * viscosity * time_step) / (0.5 * time_step)
                    mo[k, c, here, :] = (flux + m * (rise + stay)) * drain_fac[k, c]
                    uo[k, c, here, :] = (u - reward[k, c]) + (time_step * viscosity) * (
                        rise - (0.125 / viscosity) * (gr * gr + gc * gc)
                    )
                    m, u, m_back, u_back, m_from, u_from = m_next, u_next, m_next_back, u_next_back, m_on, u_on

    def out_copy(t):
        return pltpu.make_async_remote_copy(
            src_ref=out_send.at[t], dst_ref=out_recv.at[t],
            send_sem=o_ssem.at[t], recv_sem=o_rsem.at[t],
            device_id={"floor": floor - 1}, device_id_type=MESH,
        )

    def stairs(t):
        buf = M[(t + 1) % 2]
        for l in range(landings):
            face = buf[:, lm_ref[floor, 0, l], pl.ds(TOP + lm_ref[floor, 1, l], 1), :]
            out_send[t, :, l:l + 1, :] = stair_rate * face

        @pl.when(floor > 0)
        def _():
            out_copy(t).start()

    def stairs_in(t):
        @pl.when(floor > 0)
        def _():
            out_copy(t).wait_send()

        @pl.when(floor < floors - 1)
        def _():
            out_copy(t).wait_recv()

        @pl.when(floor == floors - 1)
        def _():
            out_recv[t] = jnp.zeros_like(out_recv[t])

    hm = (hm_send, hm_recv, hm_ssem, hm_rsem)
    hu = (hu_send, hu_recv, hu_ssem, hu_rsem)

    own_rk.wait()
    for off in order:
        strip_copy(rk.at[floor, me], rk.at[floor, me], rk_ssem, rk_rsem, off).start()
    for copy in small:
        copy.wait()
    for c in range(tiles):
        field_copy(dens_hbm, m0, load_m, c).wait()
    crowd_of(0, True)
    send_rims(m0, *hm, 0)
    for c in range(tiles):
        field_copy(val_hbm, u0, load_u, c).wait()
    send_rims(u0, *hu, 0)

    for off in range(1, strips):
        src = lax.rem(me + strips - off, strips)
        strip_copy(rk.at[floor, me], rk.at[floor, src], rk_ssem, rk_rsem, off).wait()
    for off in range(1, floors):
        rk_hop(off).start()

    above = jnp.minimum(floor + 1, floors - 1)
    tile_cols = width // TILES
    for tile in range(TILES):
        kind = et_ref[0, tile]
        for k in range(types):
            hit = jnp.where(kind == k, 1.0, 0.0).astype(jnp.float32)
            for c in range(tile * tile_cols // LANE, (tile + 1) * tile_cols // LANE):
                drain_fac[k, c] = jnp.full((8, LANE), (0.5 * time_step) * (1.0 - ed_ref[k] * hit), jnp.float32)
                reward[k, c] = jnp.full((8, LANE), time_step * exit_reward * hit + 8.0 * viscosity * viscosity * time_step, jnp.float32)

    stencil(0, range(1, groups - 1))

    row_at = lax.broadcasted_iota(jnp.int32, (rows, LANE), 0)

    @pl.loop(0, TILES)
    def _(tile):
        keep = jnp.ones((rows, LANE), jnp.float32)
        ids = jnp.full((rows, LANE), -1, jnp.int32)
        for l in range(landings):
            src_row = jnp.where(lm_ref[floor, 0, l] == tile, lm_ref[floor, 1, l], -1)
            dst_row = jnp.where(lm_ref[above, 2, l] == tile, lm_ref[above, 3, l], -1)
            keep = jnp.where(row_at == src_row, 1.0 - stair_rate, keep)
            ids = jnp.where(row_at == dst_row, l, ids)
        keep_map[tile] = keep
        dst_map[tile] = ids

    for t in range(SUBSTEPS):
        if t > 0:
            if t == 1:
                load_ck.wait()
            add_potential(t - 1)
            send_rims(U[t % 2], *hu, t)
            stencil(t, range(1, groups - 1))
        take_rims(M[t % 2], *hm, t)
        take_rims(U[t % 2], *hu, t)
        stencil(t, (0, groups - 1))
        stairs(t)
        if t == 0:
            for off in range(1, floors):
                rk_landed(off).wait()
        mix(t)
        stairs_in(t)
        crowd_of(t + 1, False)
        if t + 1 < SUBSTEPS:
            send_rims(M[(t + 1) % 2], *hm, t + 1)
    add_potential(SUBSTEPS - 1)
    end = SUBSTEPS % 2
    for c in range(tiles):
        here = pl.ds(c * LANE, LANE)
        pltpu.make_async_copy(M[end].at[:, c, inner, :], dens_out.at[0, :, :, here], store_m.at[c]).wait()
        pltpu.make_async_copy(U[end].at[:, c, inner, :], val_out.at[0, :, :, here], store_u.at[c]).wait()


def solution(mesh):
    strips = mesh.shape["strip"]
    floors = mesh.shape["floor"]

    def local(density, value_field, row_kernel, column_kernel, type_weight, crowd_cost, exit_drain, exit_type, landing_map):
        _, types, rows, width = density.shape
        landings = landing_map.shape[1]
        depth = row_kernel.shape[1]
        cw = width // strips
        tiles = width // LANE
        n = SUBSTEPS
        any_spec = pl.BlockSpec(memory_space=pl.ANY)
        f32, bf16 = jnp.float32, jnp.bfloat16
        dma = pltpu.SemaphoreType.DMA
        field = pltpu.VMEM((types, tiles, rows + 2 * TOP, LANE), f32)
        landing_fields = jnp.transpose(landing_map, (0, 2, 1))
        return pl.pallas_call(
            functools.partial(kernel, strips, floors, landings, types, rows, width),
            out_shape=(
                jax.ShapeDtypeStruct(density.shape, f32),
                jax.ShapeDtypeStruct(value_field.shape, f32),
            ),
            in_specs=[any_spec] * 9,
            out_specs=(any_spec, any_spec),
            scratch_shapes=[
                field,
                field,
                field,
                field,
                pltpu.VMEM(column_kernel.shape, bf16),
                pltpu.VMEM((floors, strips, rows, depth // floors), bf16),
                pltpu.VMEM((n, strips, rows, cw), bf16),
                pltpu.VMEM((n, strips, rows, cw), bf16),
                pltpu.VMEM((n, strips, rows, cw), bf16),
                pltpu.VMEM((n, strips, rows, cw), bf16),
                pltpu.VMEM((n, 2, types, tiles, LANE), f32),
                pltpu.VMEM((n, 2, types, tiles, LANE), f32),
                pltpu.VMEM((n, 2, types, tiles, LANE), f32),
                pltpu.VMEM((n, 2, types, tiles, LANE), f32),
                pltpu.VMEM((n, types, landings, LANE), f32),
                pltpu.VMEM((n, types, landings, LANE), f32),
                pltpu.VMEM((types, tiles, 8, LANE), f32),
                pltpu.VMEM((types, tiles, 8, LANE), f32),
                pltpu.VMEM((TILES, rows, LANE), f32),
                pltpu.VMEM((TILES, rows, LANE), jnp.int32),
                pltpu.SMEM(type_weight.shape, f32),
                pltpu.SMEM(crowd_cost.shape, f32),
                pltpu.SMEM(exit_drain.shape, f32),
                pltpu.SMEM(exit_type.shape, jnp.int32),
                pltpu.SMEM(landing_fields.shape, jnp.int32),
                dma((tiles,)),
                dma((tiles,)),
                dma((7,)),
                dma((tiles,)),
                dma((tiles,)),
                dma((strips,)),
                dma((strips,)),
                dma((floors,)),
                dma((floors,)),
                dma((n, strips)),
                dma((n, strips)),
                dma((n, strips)),
                dma((n, strips)),
                dma((n, 2)),
                dma((n, 2)),
                dma((n, 2)),
                dma((n, 2)),
                dma((n,)),
                dma((n,)),
            ],
            compiler_params=pltpu.CompilerParams(
                collective_id=0, has_side_effects=True, vmem_limit_bytes=52 * 1024 * 1024
            ),
        )(density, value_field, row_kernel, column_kernel, type_weight, crowd_cost, exit_drain, exit_type, landing_fields)

    placed = (
        P("floor", None, "strip", None),
        P("floor", None, "strip", None),
        P("strip", None),
        P(),
        P(),
        P(),
        P(),
        P("floor", "strip"),
        P(None, "strip", None),
    )
    return jax.shard_map(
        local,
        mesh=mesh,
        in_specs=placed,
        out_specs=(P("floor", None, "strip", None), P("floor", None, "strip", None)),
        check_vma=False,
    )
```

```python
import functools

import jax
import jax.numpy as jnp
from jax import lax
from jax.experimental import pallas as pl
from jax.experimental.pallas import tpu as pltpu
from jax.sharding import PartitionSpec as P

SUBSTEPS = 4
TILES = 16
LANE = 128
TOP = 8

time_step = 0.2
viscosity = 1.0
exit_reward = 2.0
stair_rate = 0.5

MESH = pl.DeviceIdType.MESH


def kernel(
    strips, floors, landings, types, rows, width,
    dens_hbm, val_hbm, rk_hbm, ck_hbm, tw_hbm, cc_hbm, ed_hbm, et_hbm, lm_hbm,
    dens_out, val_out,
    m0, m1, u0, u1, ck, rk, crowd_send, crowd_recv, mix_send, mix_recv,
    hm_send, hm_recv, hu_send, hu_recv, out_send, out_recv,
    drain_fac, reward, keep_map, dst_map,
    tw_ref, cc_ref, ed_ref, et_ref, lm_ref,
    load_m, load_u, load_sem, store_m, store_u, rk_ssem, rk_rsem, rf_ssem, rf_rsem,
    c_ssem, c_rsem, x_ssem, x_rsem, hm_ssem, hm_rsem, hu_ssem, hu_rsem, o_ssem, o_rsem,
):
    me = lax.axis_index("strip")
    floor = lax.axis_index("floor")
    tiles = width // LANE
    cw = width // strips
    per = cw // LANE
    groups = rows // 8
    dq = rk.shape[-1]
    inner = pl.ds(TOP, rows)
    M, U = (m0, m1), (u0, u1)

    barrier = pltpu.get_barrier_semaphore()
    for off in range(1, strips):
        pl.semaphore_signal(barrier, inc=1, device_id={"strip": lax.rem(me + off, strips)}, device_id_type=MESH)
    for off in range(1, floors):
        pl.semaphore_signal(barrier, inc=1, device_id={"floor": lax.rem(floor + off, floors)}, device_id_type=MESH)

    def field_copy(hbm, buf, sem, c):
        return pltpu.make_async_copy(hbm.at[0, :, :, pl.ds(c * LANE, LANE)], buf.at[:, c, inner, :], sem.at[c])

    for c in range(tiles):
        field_copy(dens_hbm, m0, load_m, c).start()
    my_piece = pl.ds(pl.multiple_of(floor * dq, LANE), dq)
    own_rk = pltpu.make_async_copy(rk_hbm.at[:, my_piece], rk.at[floor, me], load_sem.at[0])
    own_rk.start()
    small = [
        pltpu.make_async_copy(src, dst, load_sem.at[1 + i])
        for i, (src, dst) in enumerate(
            ((tw_hbm, tw_ref), (cc_hbm, cc_ref), (ed_hbm, ed_ref), (et_hbm, et_ref), (lm_hbm, lm_ref))
        )
    ]
    for copy in small:
        copy.start()
    for c in range(tiles):
        field_copy(val_hbm, u0, load_u, c).start()
    load_ck = pltpu.make_async_copy(ck_hbm, ck, load_sem.at[6])

    pl.semaphore_wait(barrier, strips + floors - 2)

    def strip_copy(src, dst, ssem, rsem, off):
        return pltpu.make_async_remote_copy(
            src_ref=src, dst_ref=dst, send_sem=ssem.at[off], recv_sem=rsem.at[off],
            device_id={"strip": lax.rem(me + off, strips)}, device_id_type=MESH,
        )

    def spread(step):
        return (strips // 2 + (1 - 2 * (step % 2)) * ((step + 1) // 2)) % strips

    order = [spread(step) for step in range(strips - 1)]

    def to_all(src_of, dst_ref, ssem, rsem):
        for off in order:
            strip_copy(src_of(lax.rem(me + off, strips)), dst_ref.at[me], ssem, rsem, off).start()

    def from_all(src_of, dst_ref, ssem, rsem):
        for off in range(1, strips):
            src = lax.rem(me + strips - off, strips)
            strip_copy(src_of(lax.rem(me + off, strips)), dst_ref.at[src], ssem, rsem, off).wait()

    def rk_hop(off):
        return pltpu.make_async_remote_copy(
            src_ref=rk.at[floor], dst_ref=rk.at[floor], send_sem=rf_ssem.at[off], recv_sem=rf_rsem.at[off],
            device_id={"floor": lax.rem(floor + off, floors)}, device_id_type=MESH,
        )

    def rk_landed(off):
        came = lax.rem(floor + floors - off, floors)
        return pltpu.make_async_remote_copy(
            src_ref=rk.at[floor], dst_ref=rk.at[came], send_sem=rf_ssem.at[off], recv_sem=rf_rsem.at[off],
            device_id={"floor": lax.rem(floor + off, floors)}, device_id_type=MESH,
        )

    def rim_copy(send, recv, ssem, rsem, t, side):
        return pltpu.make_async_remote_copy(
            src_ref=send.at[t, side], dst_ref=recv.at[t, 1 - side],
            send_sem=ssem.at[t, side], recv_sem=rsem.at[t, 1 - side],
            device_id={"strip": me - 1 if side == 0 else me + 1}, device_id_type=MESH,
        )

    def send_rims(buf, send, recv, ssem, rsem, t):
        def pack(side):
            at = TOP if side == 0 else TOP + rows - 1
            for k in range(types):
                row = jnp.concatenate([buf[k, c, at:at + 1, :] for c in range(tiles)], axis=0)
                send[t, side, k] = row.astype(jnp.bfloat16)
            rim_copy(send, recv, ssem, rsem, t, side).start()

        pl.when(me > 0)(lambda: pack(0))
        pl.when(me < strips - 1)(lambda: pack(1))

    def take_rims(buf, send, recv, ssem, rsem, t):
        def own(side):
            at = TOP if side == 0 else TOP + rows - 1
            to = TOP - 1 if side == 0 else TOP + rows
            for k in range(types):
                for c in range(tiles):
                    buf[k, c, to:to + 1, :] = buf[k, c, at:at + 1, :]

        def got(side):
            rim_copy(send, recv, ssem, rsem, t, side).wait_send()
            pltpu.make_async_remote_copy(
                src_ref=send.at[t, side], dst_ref=recv.at[t, side],
                send_sem=ssem.at[t, side], recv_sem=rsem.at[t, side],
                device_id={"strip": me - 1 if side == 0 else me + 1}, device_id_type=MESH,
            ).wait_recv()
            to = TOP - 1 if side == 0 else TOP + rows
            for k in range(types):
                row = recv[t, side, k].astype(jnp.float32)
                for c in range(tiles):
                    buf[k, c, to:to + 1, :] = row[c:c + 1, :]

        pl.when(me > 0)(lambda: got(0))
        pl.when(me == 0)(lambda: own(0))
        pl.when(me < strips - 1)(lambda: got(1))
        pl.when(me == strips - 1)(lambda: own(1))

    def crowd_of(t, initial):
        buf = M[t % 2]

        @pl.loop(0, strips)
        def _(step):
            off = lax.rem(strips // 2 + (1 - 2 * lax.rem(step, 2)) * lax.div(step + 1, 2), strips)
            dst = lax.rem(me + off, strips)
            for q in range(per):
                c = dst * per + q
                total = None
                if not initial:
                    keep = keep_map[c]
                    ids = dst_map[c]
                    slot = jnp.maximum(ids, 0)
                    landed = ids >= 0
                for k in range(types):
                    v = buf[k, c, inner, :]
                    if not initial:
                        if landings == 8:
                            add = jnp.concatenate([
                                jnp.take_along_axis(out_recv[t - 1, k], slot[r:r + 8], axis=0, mode="promise_in_bounds")
                                for r in range(0, rows, 8)
                            ], axis=0)
                            add = jnp.where(landed, add, 0.0)
                        else:
                            add = jnp.zeros_like(v)
                            for l in range(landings):
                                add = jnp.where(ids == l, out_recv[t - 1, k, l:l + 1, :], add)
                        v = v * keep + add
                        buf[k, c, inner, :] = v
                    term = tw_ref[k] * v
                    total = term if total is None else total + term
                if t < SUBSTEPS:
                    crowd_send[t, dst, :, q * LANE:(q + 1) * LANE] = total.astype(jnp.bfloat16)
                else:
                    pltpu.make_async_copy(
                        buf.at[:, c, inner, :],
                        dens_out.at[0, :, :, pl.ds(pl.multiple_of(c * LANE, LANE), LANE)],
                        store_m.at[c],
                    ).start()
            if t < SUBSTEPS:
                @pl.when(off > 0)
                def _():
                    strip_copy(crowd_send.at[t, dst], crowd_recv.at[t, me], c_ssem.at[t], c_rsem.at[t], off).start()

        if t < SUBSTEPS:
            crowd_recv[t, me] = crowd_send[t, me]

    def mix(t):
        from_all(lambda d: crowd_send.at[t, d], crowd_recv.at[t], c_ssem.at[t], c_rsem.at[t])
        crowd = crowd_recv[t].reshape(strips * rows, cw)
        weights = jnp.concatenate([rk[q].reshape(strips * rows, dq) for q in range(floors)], axis=1)
        mixed = jnp.dot(weights, crowd, preferred_element_type=jnp.float32)
        mix_send[t] = mixed.astype(jnp.bfloat16).reshape(strips, rows, cw)
        to_all(lambda d: mix_send.at[t, d], mix_recv.at[t], x_ssem.at[t], x_rsem.at[t])
        mix_recv[t, me] = mix_send[t, me]

    def add_potential(t):
        buf = U[(t + 1) % 2]
        from_all(lambda d: mix_send.at[t, d], mix_recv.at[t], x_ssem.at[t], x_rsem.at[t])
        step = 4 * LANE

        @pl.loop(0, width // step)
        def _(n):
            start = pl.multiple_of(n * step, step)
            acc = None
            for s in range(strips):
                d = jnp.dot(mix_recv[t, s], ck[s * cw:(s + 1) * cw, pl.ds(start, step)], preferred_element_type=jnp.float32)
                acc = d if acc is None else acc + d
            for q in range(4):
                c = 4 * n + q
                part = acc[:, q * LANE:(q + 1) * LANE]
                for k in range(types):
                    buf[k, c, inner, :] = buf[k, c, inner, :] + (time_step * cc_ref[k]) * part
                if t == SUBSTEPS - 1:
                    pltpu.make_async_copy(
                        buf.at[:, c, inner, :],
                        val_out.at[0, :, :, pl.ds(pl.multiple_of(c * LANE, LANE), LANE)],
                        store_u.at[c],
                    ).start()

    lane = lax.broadcasted_iota(jnp.int32, (8, LANE), 1)
    first, last = lane == 0, lane == LANE - 1

    def stencil(t, chunks):
        mb, ub, mo, uo = M[t % 2], U[t % 2], M[(t + 1) % 2], U[(t + 1) % 2]

        @pl.loop(0, types)
        def _(k):
            for r in chunks:
                lo = TOP + 8 * r
                here = slice(lo, lo + 8)
                m, u = mb[k, 0, here, :], ub[k, 0, here, :]
                m_from, u_from = m, u
                m_back, u_back = pltpu.roll(m, LANE - 1, 1), pltpu.roll(u, LANE - 1, 1)
                for c in range(tiles):
                    if c < tiles - 1:
                        m_next, u_next = mb[k, c + 1, here, :], ub[k, c + 1, here, :]
                        m_next_back, u_next_back = pltpu.roll(m_next, LANE - 1, 1), pltpu.roll(u_next, LANE - 1, 1)
                    else:
                        m_next, u_next, m_next_back, u_next_back = m, u, m, u
                    mr, ur = jnp.where(last, m_next_back, m_back), jnp.where(last, u_next_back, u_back)
                    m_on, u_on = pltpu.roll(m, 1, 1), pltpu.roll(u, 1, 1)
                    ml, ul = jnp.where(first, m_from, m_on), jnp.where(first, u_from, u_on)
                    mu, md = mb[k, c, lo - 1:lo + 7, :], mb[k, c, lo + 1:lo + 9, :]
                    uu, ud = ub[k, c, lo - 1:lo + 7, :], ub[k, c, lo + 1:lo + 9, :]
                    low = u - 2.0 * viscosity
                    flux = None
                    rise = None
                    for mn, un in ((mu, uu), (md, ud), (ml, ul), (mr, ur)):
                        p = un - low
                        flux = mn * p if flux is None else flux + mn * p
                        rise = p if rise is None else rise + p
                    gr = ud - uu
                    gc = ur - ul
                    stay = (1.0 - 8.0 * viscosity * time_step) / (0.5 * time_step)
                    mo[k, c, here, :] = (flux + m * (rise + stay)) * drain_fac[k, c]
                    uo[k, c, here, :] = (u - reward[k, c]) + (time_step * viscosity) * (
                        rise - (0.125 / viscosity) * (gr * gr + gc * gc)
                    )
                    m, u, m_back, u_back, m_from, u_from = m_next, u_next, m_next_back, u_next_back, m_on, u_on

    def out_copy(t):
        return pltpu.make_async_remote_copy(
            src_ref=out_send.at[t], dst_ref=out_recv.at[t],
            send_sem=o_ssem.at[t], recv_sem=o_rsem.at[t],
            device_id={"floor": floor - 1}, device_id_type=MESH,
        )

    def stairs(t):
        buf = M[(t + 1) % 2]
        for l in range(landings):
            face = buf[:, lm_ref[floor, 0, l], pl.ds(TOP + lm_ref[floor, 1, l], 1), :]
            out_send[t, :, l:l + 1, :] = stair_rate * face

        @pl.when(floor > 0)
        def _():
            out_copy(t).start()

    def stairs_in(t):
        @pl.when(floor > 0)
        def _():
            out_copy(t).wait_send()

        @pl.when(floor < floors - 1)
        def _():
            out_copy(t).wait_recv()

        @pl.when(floor == floors - 1)
        def _():
            out_recv[t] = jnp.zeros_like(out_recv[t])

    hm = (hm_send, hm_recv, hm_ssem, hm_rsem)
    hu = (hu_send, hu_recv, hu_ssem, hu_rsem)

    own_rk.wait()
    for off in order:
        strip_copy(rk.at[floor, me], rk.at[floor, me], rk_ssem, rk_rsem, off).start()
    for copy in small:
        copy.wait()
    for c in range(tiles):
        field_copy(dens_hbm, m0, load_m, c).wait()
    crowd_of(0, True)
    load_ck.start()
    send_rims(m0, *hm, 0)
    for c in range(tiles):
        field_copy(val_hbm, u0, load_u, c).wait()
    send_rims(u0, *hu, 0)

    for off in range(1, strips):
        src = lax.rem(me + strips - off, strips)
        strip_copy(rk.at[floor, me], rk.at[floor, src], rk_ssem, rk_rsem, off).wait()
    for off in range(1, floors):
        rk_hop(off).start()

    above = jnp.minimum(floor + 1, floors - 1)
    tile_cols = width // TILES
    for tile in range(TILES):
        kind = et_ref[0, tile]
        for k in range(types):
            hit = jnp.where(kind == k, 1.0, 0.0).astype(jnp.float32)
            for c in range(tile * tile_cols // LANE, (tile + 1) * tile_cols // LANE):
                drain_fac[k, c] = jnp.full((8, LANE), (0.5 * time_step) * (1.0 - ed_ref[k] * hit), jnp.float32)
                reward[k, c] = jnp.full((8, LANE), time_step * exit_reward * hit + 8.0 * viscosity * viscosity * time_step, jnp.float32)

    stencil(0, range(1, groups - 1))

    row_at = lax.broadcasted_iota(jnp.int32, (rows, LANE), 0)

    @pl.loop(0, TILES)
    def _(tile):
        keep = jnp.ones((rows, LANE), jnp.float32)
        ids = jnp.full((rows, LANE), -1, jnp.int32)
        for l in range(landings):
            src_row = jnp.where(lm_ref[floor, 0, l] == tile, lm_ref[floor, 1, l], -1)
            dst_row = jnp.where(lm_ref[above, 2, l] == tile, lm_ref[above, 3, l], -1)
            keep = jnp.where(row_at == src_row, 1.0 - stair_rate, keep)
            ids = jnp.where(row_at == dst_row, l, ids)
        keep_map[tile] = keep
        dst_map[tile] = ids

    for t in range(SUBSTEPS):
        if t > 0:
            if t == 1:
                load_ck.wait()
            add_potential(t - 1)
            send_rims(U[t % 2], *hu, t)
            stencil(t, range(1, groups - 1))
        if t == 0:
            for off in range(1, floors):
                rk_landed(off).wait()
        mix(t)
        take_rims(M[t % 2], *hm, t)
        take_rims(U[t % 2], *hu, t)
        stencil(t, (0, groups - 1))
        stairs(t)
        stairs_in(t)
        crowd_of(t + 1, False)
        if t + 1 < SUBSTEPS:
            send_rims(M[(t + 1) % 2], *hm, t + 1)
    add_potential(SUBSTEPS - 1)
    end = SUBSTEPS % 2
    for c in range(tiles):
        here = pl.ds(c * LANE, LANE)
        pltpu.make_async_copy(M[end].at[:, c, inner, :], dens_out.at[0, :, :, here], store_m.at[c]).wait()
        pltpu.make_async_copy(U[end].at[:, c, inner, :], val_out.at[0, :, :, here], store_u.at[c]).wait()


def finish(m_in, u_in, m_out, u_out, held, in_sem, out_sem):
    into, out = [], []
    for i, (src, dst) in enumerate(((m_in, m_out), (u_in, u_out))):
        for k in range(src.shape[1]):
            into.append(pltpu.make_async_copy(src.at[0, k], held.at[i, k], in_sem.at[i, k]))
            out.append(pltpu.make_async_copy(held.at[i, k], dst.at[0, k], out_sem.at[i, k]))
    for copy in into:
        copy.start()
    for came, leaves in zip(into, out):
        came.wait()
        leaves.start()
    for copy in out:
        copy.wait()


def solution(mesh):
    strips = mesh.shape["strip"]
    floors = mesh.shape["floor"]

    def local(density, value_field, row_kernel, column_kernel, type_weight, crowd_cost, exit_drain, exit_type, landing_map):
        _, types, rows, width = density.shape
        landings = landing_map.shape[1]
        depth = row_kernel.shape[1]
        cw = width // strips
        tiles = width // LANE
        n = SUBSTEPS
        any_spec = pl.BlockSpec(memory_space=pltpu.HBM)
        f32, bf16 = jnp.float32, jnp.bfloat16
        dma = pltpu.SemaphoreType.DMA
        field = pltpu.VMEM((types, tiles, rows + 2 * TOP, LANE), f32)
        landing_fields = jnp.transpose(landing_map, (0, 2, 1))
        new = pl.pallas_call(
            functools.partial(kernel, strips, floors, landings, types, rows, width),
            out_shape=(
                jax.ShapeDtypeStruct(density.shape, f32),
                jax.ShapeDtypeStruct(value_field.shape, f32),
            ),
            in_specs=[any_spec] * 9,
            out_specs=(any_spec, any_spec),
            scratch_shapes=[
                field,
                field,
                field,
                field,
                pltpu.VMEM(column_kernel.shape, bf16),
                pltpu.VMEM((floors, strips, rows, depth // floors), bf16),
                pltpu.VMEM((n, strips, rows, cw), bf16),
                pltpu.VMEM((n, strips, rows, cw), bf16),
                pltpu.VMEM((n, strips, rows, cw), bf16),
                pltpu.VMEM((n, strips, rows, cw), bf16),
                pltpu.VMEM((n, 2, types, tiles, LANE), bf16),
                pltpu.VMEM((n, 2, types, tiles, LANE), bf16),
                pltpu.VMEM((n, 2, types, tiles, LANE), bf16),
                pltpu.VMEM((n, 2, types, tiles, LANE), bf16),
                pltpu.VMEM((n, types, landings, LANE), f32),
                pltpu.VMEM((n, types, landings, LANE), f32),
                pltpu.VMEM((types, tiles, 8, LANE), f32),
                pltpu.VMEM((types, tiles, 8, LANE), f32),
                pltpu.VMEM((TILES, rows, LANE), f32),
                pltpu.VMEM((TILES, rows, LANE), jnp.int32),
                pltpu.SMEM(type_weight.shape, f32),
                pltpu.SMEM(crowd_cost.shape, f32),
                pltpu.SMEM(exit_drain.shape, f32),
                pltpu.SMEM(exit_type.shape, jnp.int32),
                pltpu.SMEM(landing_fields.shape, jnp.int32),
                dma((tiles,)),
                dma((tiles,)),
                dma((7,)),
                dma((tiles,)),
                dma((tiles,)),
                dma((strips,)),
                dma((strips,)),
                dma((floors,)),
                dma((floors,)),
                dma((n, strips)),
                dma((n, strips)),
                dma((n, strips)),
                dma((n, strips)),
                dma((n, 2)),
                dma((n, 2)),
                dma((n, 2)),
                dma((n, 2)),
                dma((n,)),
                dma((n,)),
            ],
            compiler_params=pltpu.CompilerParams(
                collective_id=0, has_side_effects=True, vmem_limit_bytes=64 * 1024 * 1024
            ),
        )(density, value_field, row_kernel, column_kernel, type_weight, crowd_cost, exit_drain, exit_type, landing_fields)
        return pl.pallas_call(
            finish,
            out_shape=(
                jax.ShapeDtypeStruct(density.shape, f32),
                jax.ShapeDtypeStruct(value_field.shape, f32),
            ),
            in_specs=[any_spec] * 2,
            out_specs=(any_spec, any_spec),
            scratch_shapes=[pltpu.VMEM((2, types, rows, width), f32), dma((2, types)), dma((2, types))],
            compiler_params=pltpu.CompilerParams(vmem_limit_bytes=64 * 1024 * 1024),
        )(*new)

    placed = (
        P("floor", None, "strip", None),
        P("floor", None, "strip", None),
        P("strip", None),
        P(),
        P(),
        P(),
        P(),
        P("floor", "strip"),
        P(None, "strip", None),
    )
    return jax.shard_map(
        local,
        mesh=mesh,
        in_specs=placed,
        out_specs=(P("floor", None, "strip", None), P("floor", None, "strip", None)),
        check_vma=False,
    )
```

```python
import functools

import jax
import jax.numpy as jnp
from jax import lax
from jax.experimental import pallas as pl
from jax.experimental.pallas import tpu as pltpu
from jax.sharding import PartitionSpec as P

SUBSTEPS = 4
TILES = 16
LANE = 128
TOP = 8

time_step = 0.2
viscosity = 1.0
exit_reward = 2.0
stair_rate = 0.5

MESH = pl.DeviceIdType.MESH


def kernel(
    strips, floors, landings, types, rows, width,
    dens_hbm, val_hbm, rk_hbm, ck_hbm, tw_hbm, cc_hbm, ed_hbm, et_hbm, lm_hbm,
    dens_out, val_out,
    m0, m1, u0, u1, ck, rk, crowd_send, crowd_recv, mix_send, mix_recv,
    hm_send, hm_recv, hu_send, hu_recv, out_send, out_recv,
    drain_fac, reward, keep_map, dst_map, rk_own,
    tw_ref, cc_ref, ed_ref, et_ref, lm_ref,
    load_m, load_u, load_sem, store_m, store_u, rk_ssem, rk_rsem, rf_ssem, rf_rsem, rm_ssem, rm_rsem,
    c_ssem, c_rsem, x_ssem, x_rsem, hm_ssem, hm_rsem, hu_ssem, hu_rsem, o_ssem, o_rsem,
):
    me = lax.axis_index("strip")
    floor = lax.axis_index("floor")
    tiles = width // LANE
    cw = width // strips
    per = cw // LANE
    groups = rows // 8
    dq = rk.shape[-1]
    half = rows // 2
    core = lax.rem(me, 2)
    inner = pl.ds(TOP, rows)
    M, U = (m0, m1), (u0, u1)

    barrier = pltpu.get_barrier_semaphore()
    for off in range(1, strips):
        pl.semaphore_signal(barrier, inc=1, device_id={"strip": lax.rem(me + off, strips)}, device_id_type=MESH)
    for off in range(1, floors):
        pl.semaphore_signal(barrier, inc=1, device_id={"floor": lax.rem(floor + off, floors)}, device_id_type=MESH)

    def field_copy(hbm, buf, sem, c):
        return pltpu.make_async_copy(hbm.at[0, :, :, pl.ds(c * LANE, LANE)], buf.at[:, c, inner, :], sem.at[c])

    for c in range(tiles):
        field_copy(dens_hbm, m0, load_m, c).start()
    my_piece = pl.ds(pl.multiple_of(floor * dq, LANE), dq)
    own_rk = pltpu.make_async_copy(rk_hbm.at[:, my_piece], rk_own, load_sem.at[0])
    own_rk.start()
    small = [
        pltpu.make_async_copy(src, dst, load_sem.at[1 + i])
        for i, (src, dst) in enumerate(
            ((tw_hbm, tw_ref), (cc_hbm, cc_ref), (ed_hbm, ed_ref), (et_hbm, et_ref), (lm_hbm, lm_ref))
        )
    ]
    for copy in small:
        copy.start()
    for c in range(tiles):
        field_copy(val_hbm, u0, load_u, c).start()
    load_ck = pltpu.make_async_copy(ck_hbm, ck, load_sem.at[6])

    pl.semaphore_wait(barrier, strips + floors - 2)

    def strip_copy(src, dst, ssem, rsem, off):
        return pltpu.make_async_remote_copy(
            src_ref=src, dst_ref=dst, send_sem=ssem.at[off], recv_sem=rsem.at[off],
            device_id={"strip": lax.rem(me + off, strips)}, device_id_type=MESH,
        )

    def spread(step):
        return (strips // 2 + (1 - 2 * (step % 2)) * ((step + 1) // 2)) % strips

    order = [spread(step) for step in range(strips - 1)]

    def to_all(src_of, dst_ref, ssem, rsem):
        for off in order:
            strip_copy(src_of(lax.rem(me + off, strips)), dst_ref.at[me], ssem, rsem, off).start()

    def from_all(src_of, dst_ref, ssem, rsem):
        for off in range(1, strips):
            src = lax.rem(me + strips - off, strips)
            strip_copy(src_of(lax.rem(me + off, strips)), dst_ref.at[src], ssem, rsem, off).wait()

    def rk_hop(off):
        return pltpu.make_async_remote_copy(
            src_ref=rk.at[floor, core], dst_ref=rk.at[floor, core], send_sem=rf_ssem.at[off], recv_sem=rf_rsem.at[off],
            device_id={"floor": lax.rem(floor + off, floors)}, device_id_type=MESH,
        )

    def rk_landed(off):
        came = lax.rem(floor + floors - off, floors)
        return pltpu.make_async_remote_copy(
            src_ref=rk.at[floor, core], dst_ref=rk.at[came, core], send_sem=rf_ssem.at[off], recv_sem=rf_rsem.at[off],
            device_id={"floor": lax.rem(floor + off, floors)}, device_id_type=MESH,
        )

    def rk_mate(f, side):
        return pltpu.make_async_remote_copy(
            src_ref=rk.at[f, core], dst_ref=rk.at[f, side], send_sem=rm_ssem.at[f], recv_sem=rm_rsem.at[f],
            device_id={"strip": me + 1 - 2 * core}, device_id_type=MESH,
        )

    def rk_share(off, slot):
        side = lax.rem(lax.rem(me + off, strips), 2)
        rows_for = rk_own.at[pl.ds(pl.multiple_of(side * half, half), half), :]
        return strip_copy(rows_for, slot(side), rk_ssem, rk_rsem, off)

    def rim_copy(send, recv, ssem, rsem, t, side):
        return pltpu.make_async_remote_copy(
            src_ref=send.at[t, side], dst_ref=recv.at[t, 1 - side],
            send_sem=ssem.at[t, side], recv_sem=rsem.at[t, 1 - side],
            device_id={"strip": me - 1 if side == 0 else me + 1}, device_id_type=MESH,
        )

    def send_rims(buf, send, recv, ssem, rsem, t):
        def pack(side):
            at = TOP if side == 0 else TOP + rows - 1
            for k in range(types):
                row = jnp.concatenate([buf[k, c, at:at + 1, :] for c in range(tiles)], axis=0)
                send[t, side, k] = row.astype(jnp.bfloat16)
            rim_copy(send, recv, ssem, rsem, t, side).start()

        pl.when(me > 0)(lambda: pack(0))
        pl.when(me < strips - 1)(lambda: pack(1))

    def take_rims(buf, send, recv, ssem, rsem, t):
        def own(side):
            at = TOP if side == 0 else TOP + rows - 1
            to = TOP - 1 if side == 0 else TOP + rows
            for k in range(types):
                for c in range(tiles):
                    buf[k, c, to:to + 1, :] = buf[k, c, at:at + 1, :]

        def got(side):
            rim_copy(send, recv, ssem, rsem, t, side).wait_send()
            pltpu.make_async_remote_copy(
                src_ref=send.at[t, side], dst_ref=recv.at[t, side],
                send_sem=ssem.at[t, side], recv_sem=rsem.at[t, side],
                device_id={"strip": me - 1 if side == 0 else me + 1}, device_id_type=MESH,
            ).wait_recv()
            to = TOP - 1 if side == 0 else TOP + rows
            for k in range(types):
                row = recv[t, side, k].astype(jnp.float32)
                for c in range(tiles):
                    buf[k, c, to:to + 1, :] = row[c:c + 1, :]

        pl.when(me > 0)(lambda: got(0))
        pl.when(me == 0)(lambda: own(0))
        pl.when(me < strips - 1)(lambda: got(1))
        pl.when(me == strips - 1)(lambda: own(1))

    def crowd_of(t, initial):
        buf = M[t % 2]

        @pl.loop(0, strips)
        def _(step):
            off = lax.rem(strips // 2 + (1 - 2 * lax.rem(step, 2)) * lax.div(step + 1, 2), strips)
            dst = lax.rem(me + off, strips)
            for q in range(per):
                c = dst * per + q
                total = None
                if not initial:
                    keep = keep_map[c]
                    ids = dst_map[c]
                    slot = jnp.maximum(ids, 0)
                    landed = ids >= 0
                for k in range(types):
                    v = buf[k, c, inner, :]
                    if not initial:
                        if landings == 8:
                            add = jnp.concatenate([
                                jnp.take_along_axis(out_recv[t - 1, k], slot[r:r + 8], axis=0, mode="promise_in_bounds")
                                for r in range(0, rows, 8)
                            ], axis=0)
                            add = jnp.where(landed, add, 0.0)
                        else:
                            add = jnp.zeros_like(v)
                            for l in range(landings):
                                add = jnp.where(ids == l, out_recv[t - 1, k, l:l + 1, :], add)
                        v = v * keep + add
                        buf[k, c, inner, :] = v
                    term = tw_ref[k] * v
                    total = term if total is None else total + term
                if t < SUBSTEPS:
                    crowd_send[t, dst, :, q * LANE:(q + 1) * LANE] = total.astype(jnp.bfloat16)
                else:
                    pltpu.make_async_copy(
                        buf.at[:, c, inner, :],
                        dens_out.at[0, :, :, pl.ds(pl.multiple_of(c * LANE, LANE), LANE)],
                        store_m.at[c],
                    ).start()
            if t < SUBSTEPS:
                @pl.when(off > 0)
                def _():
                    strip_copy(crowd_send.at[t, dst], crowd_recv.at[t, me], c_ssem.at[t], c_rsem.at[t], off).start()

        if t < SUBSTEPS:
            crowd_recv[t, me] = crowd_send[t, me]

    def mix(t):
        from_all(lambda d: crowd_send.at[t, d], crowd_recv.at[t], c_ssem.at[t], c_rsem.at[t])
        crowd = crowd_recv[t].reshape(strips * rows, cw)
        group = strips // 2
        far = (1 - lax.div(me, group)) * group
        for base in (far, group - far):
            weights = jnp.concatenate([
                jnp.concatenate([rk[f, h, pl.ds(base, group)].reshape(group * half, dq) for f in range(floors)], axis=1)
                for h in range(2)
            ], axis=0)
            mixed = jnp.dot(weights, crowd, preferred_element_type=jnp.float32).astype(jnp.bfloat16)
            for h in range(2):
                mix_send[t, pl.ds(base, group), h * half:(h + 1) * half, :] = (
                    mixed[h * group * half:(h + 1) * group * half].reshape(group, half, cw)
                )
            for i in range(group):
                off = lax.rem(base + lax.rem(me + i, group) - me + strips, strips)

                @pl.when(off > 0)
                def _():
                    strip_copy(mix_send.at[t, lax.rem(me + off, strips)], mix_recv.at[t, me], x_ssem.at[t], x_rsem.at[t], off).start()
        mix_recv[t, me] = mix_send[t, me]

    def add_potential(t):
        buf = U[(t + 1) % 2]
        from_all(lambda d: mix_send.at[t, d], mix_recv.at[t], x_ssem.at[t], x_rsem.at[t])
        step = 4 * LANE

        @pl.loop(0, width // step)
        def _(n):
            start = pl.multiple_of(n * step, step)
            acc = None
            for s in range(strips):
                d = jnp.dot(mix_recv[t, s], ck[s * cw:(s + 1) * cw, pl.ds(start, step)], preferred_element_type=jnp.float32)
                acc = d if acc is None else acc + d
            for q in range(4):
                c = 4 * n + q
                part = acc[:, q * LANE:(q + 1) * LANE]
                for k in range(types):
                    buf[k, c, inner, :] = buf[k, c, inner, :] + (time_step * cc_ref[k]) * part
                if t == SUBSTEPS - 1:
                    pltpu.make_async_copy(
                        buf.at[:, c, inner, :],
                        val_out.at[0, :, :, pl.ds(pl.multiple_of(c * LANE, LANE), LANE)],
                        store_u.at[c],
                    ).start()

    lane = lax.broadcasted_iota(jnp.int32, (8, LANE), 1)
    first, last = lane == 0, lane == LANE - 1

    def stencil(t, chunks):
        mb, ub, mo, uo = M[t % 2], U[t % 2], M[(t + 1) % 2], U[(t + 1) % 2]

        @pl.loop(0, types)
        def _(k):
            for r in chunks:
                lo = TOP + 8 * r
                here = slice(lo, lo + 8)
                m, u = mb[k, 0, here, :], ub[k, 0, here, :]
                m_from, u_from = m, u
                m_back, u_back = pltpu.roll(m, LANE - 1, 1), pltpu.roll(u, LANE - 1, 1)
                for c in range(tiles):
                    if c < tiles - 1:
                        m_next, u_next = mb[k, c + 1, here, :], ub[k, c + 1, here, :]
                        m_next_back, u_next_back = pltpu.roll(m_next, LANE - 1, 1), pltpu.roll(u_next, LANE - 1, 1)
                    else:
                        m_next, u_next, m_next_back, u_next_back = m, u, m, u
                    mr, ur = jnp.where(last, m_next_back, m_back), jnp.where(last, u_next_back, u_back)
                    m_on, u_on = pltpu.roll(m, 1, 1), pltpu.roll(u, 1, 1)
                    ml, ul = jnp.where(first, m_from, m_on), jnp.where(first, u_from, u_on)
                    mu, md = mb[k, c, lo - 1:lo + 7, :], mb[k, c, lo + 1:lo + 9, :]
                    uu, ud = ub[k, c, lo - 1:lo + 7, :], ub[k, c, lo + 1:lo + 9, :]
                    low = u - 2.0 * viscosity
                    flux = None
                    rise = None
                    for mn, un in ((mu, uu), (md, ud), (ml, ul), (mr, ur)):
                        p = un - low
                        flux = mn * p if flux is None else flux + mn * p
                        rise = p if rise is None else rise + p
                    gr = ud - uu
                    gc = ur - ul
                    stay = (1.0 - 8.0 * viscosity * time_step) / (0.5 * time_step)
                    mo[k, c, here, :] = (flux + m * (rise + stay)) * drain_fac[k, c]
                    uo[k, c, here, :] = (u - reward[k, c]) + (time_step * viscosity) * (
                        rise - (0.125 / viscosity) * (gr * gr + gc * gc)
                    )
                    m, u, m_back, u_back, m_from, u_from = m_next, u_next, m_next_back, u_next_back, m_on, u_on

    def out_copy(t):
        return pltpu.make_async_remote_copy(
            src_ref=out_send.at[t], dst_ref=out_recv.at[t],
            send_sem=o_ssem.at[t], recv_sem=o_rsem.at[t],
            device_id={"floor": floor - 1}, device_id_type=MESH,
        )

    def stairs(t):
        buf = M[(t + 1) % 2]
        for l in range(landings):
            face = buf[:, lm_ref[floor, 0, l], pl.ds(TOP + lm_ref[floor, 1, l], 1), :]
            out_send[t, :, l:l + 1, :] = stair_rate * face

        @pl.when(floor > 0)
        def _():
            out_copy(t).start()

    def stairs_in(t):
        @pl.when(floor > 0)
        def _():
            out_copy(t).wait_send()

        @pl.when(floor < floors - 1)
        def _():
            out_copy(t).wait_recv()

        @pl.when(floor == floors - 1)
        def _():
            out_recv[t] = jnp.zeros_like(out_recv[t])

    hm = (hm_send, hm_recv, hm_ssem, hm_rsem)
    hu = (hu_send, hu_recv, hu_ssem, hu_rsem)

    own_rk.wait()
    for off in order:
        rk_share(off, lambda side: rk.at[floor, side, me]).start()
    for copy in small:
        copy.wait()
    for c in range(tiles):
        field_copy(dens_hbm, m0, load_m, c).wait()
    crowd_of(0, True)
    load_ck.start()
    send_rims(m0, *hm, 0)
    for c in range(tiles):
        field_copy(val_hbm, u0, load_u, c).wait()
    send_rims(u0, *hu, 0)

    for off in range(1, strips):
        src = lax.rem(me + strips - off, strips)
        rk_share(off, lambda side: rk.at[floor, core, src]).wait()
    rk[floor, core, me] = rk_own[pl.ds(pl.multiple_of(core * half, half), half), :]
    for off in range(1, floors):
        rk_hop(off).start()
    rk_mate(floor, core).start()

    above = jnp.minimum(floor + 1, floors - 1)
    tile_cols = width // TILES
    for tile in range(TILES):
        kind = et_ref[0, tile]
        for k in range(types):
            hit = jnp.where(kind == k, 1.0, 0.0).astype(jnp.float32)
            for c in range(tile * tile_cols // LANE, (tile + 1) * tile_cols // LANE):
                drain_fac[k, c] = jnp.full((8, LANE), (0.5 * time_step) * (1.0 - ed_ref[k] * hit), jnp.float32)
                reward[k, c] = jnp.full((8, LANE), time_step * exit_reward * hit + 8.0 * viscosity * viscosity * time_step, jnp.float32)

    stencil(0, range(1, groups - 1))

    for off in range(1, floors):
        rk_landed(off).wait()
        rk_mate(lax.rem(floor + floors - off, floors), core).start()

    row_at = lax.broadcasted_iota(jnp.int32, (rows, LANE), 0)

    @pl.loop(0, TILES)
    def _(tile):
        keep = jnp.ones((rows, LANE), jnp.float32)
        ids = jnp.full((rows, LANE), -1, jnp.int32)
        for l in range(landings):
            src_row = jnp.where(lm_ref[floor, 0, l] == tile, lm_ref[floor, 1, l], -1)
            dst_row = jnp.where(lm_ref[above, 2, l] == tile, lm_ref[above, 3, l], -1)
            keep = jnp.where(row_at == src_row, 1.0 - stair_rate, keep)
            ids = jnp.where(row_at == dst_row, l, ids)
        keep_map[tile] = keep
        dst_map[tile] = ids

    for t in range(SUBSTEPS):
        if t > 0:
            if t == 1:
                load_ck.wait()
            add_potential(t - 1)
            send_rims(U[t % 2], *hu, t)
            stencil(t, range(1, groups - 1))
        if t == 0:
            for f in range(floors):
                rk_mate(f, 1 - core).wait()
        mix(t)
        take_rims(M[t % 2], *hm, t)
        take_rims(U[t % 2], *hu, t)
        stencil(t, (0, groups - 1))
        stairs(t)
        stairs_in(t)
        crowd_of(t + 1, False)
        if t + 1 < SUBSTEPS:
            send_rims(M[(t + 1) % 2], *hm, t + 1)
    add_potential(SUBSTEPS - 1)
    end = SUBSTEPS % 2
    for c in range(tiles):
        here = pl.ds(c * LANE, LANE)
        pltpu.make_async_copy(M[end].at[:, c, inner, :], dens_out.at[0, :, :, here], store_m.at[c]).wait()
        pltpu.make_async_copy(U[end].at[:, c, inner, :], val_out.at[0, :, :, here], store_u.at[c]).wait()


def finish(m_in, u_in, m_out, u_out, held, in_sem, out_sem):
    into, out = [], []
    for i, (src, dst) in enumerate(((m_in, m_out), (u_in, u_out))):
        for k in range(src.shape[1]):
            into.append(pltpu.make_async_copy(src.at[0, k], held.at[i, k], in_sem.at[i, k]))
            out.append(pltpu.make_async_copy(held.at[i, k], dst.at[0, k], out_sem.at[i, k]))
    for copy in into:
        copy.start()
    for came, leaves in zip(into, out):
        came.wait()
        leaves.start()
    for copy in out:
        copy.wait()


def solution(mesh):
    strips = mesh.shape["strip"]
    floors = mesh.shape["floor"]

    def local(density, value_field, row_kernel, column_kernel, type_weight, crowd_cost, exit_drain, exit_type, landing_map):
        _, types, rows, width = density.shape
        landings = landing_map.shape[1]
        depth = row_kernel.shape[1]
        cw = width // strips
        tiles = width // LANE
        n = SUBSTEPS
        any_spec = pl.BlockSpec(memory_space=pltpu.HBM)
        f32, bf16 = jnp.float32, jnp.bfloat16
        dma = pltpu.SemaphoreType.DMA
        field = pltpu.VMEM((types, tiles, rows + 2 * TOP, LANE), f32)
        landing_fields = jnp.transpose(landing_map, (0, 2, 1))
        new = pl.pallas_call(
            functools.partial(kernel, strips, floors, landings, types, rows, width),
            out_shape=(
                jax.ShapeDtypeStruct(density.shape, f32),
                jax.ShapeDtypeStruct(value_field.shape, f32),
            ),
            in_specs=[any_spec] * 9,
            out_specs=(any_spec, any_spec),
            scratch_shapes=[
                field,
                field,
                field,
                field,
                pltpu.VMEM(column_kernel.shape, bf16),
                pltpu.VMEM((floors, 2, strips, rows // 2, depth // floors), bf16),
                pltpu.VMEM((n, strips, rows, cw), bf16),
                pltpu.VMEM((n, strips, rows, cw), bf16),
                pltpu.VMEM((n, strips, rows, cw), bf16),
                pltpu.VMEM((n, strips, rows, cw), bf16),
                pltpu.VMEM((n, 2, types, tiles, LANE), bf16),
                pltpu.VMEM((n, 2, types, tiles, LANE), bf16),
                pltpu.VMEM((n, 2, types, tiles, LANE), bf16),
                pltpu.VMEM((n, 2, types, tiles, LANE), bf16),
                pltpu.VMEM((n, types, landings, LANE), f32),
                pltpu.VMEM((n, types, landings, LANE), f32),
                pltpu.VMEM((types, tiles, 8, LANE), f32),
                pltpu.VMEM((types, tiles, 8, LANE), f32),
                pltpu.VMEM((TILES, rows, LANE), f32),
                pltpu.VMEM((TILES, rows, LANE), jnp.int32),
                pltpu.VMEM((rows, depth // floors), bf16),
                pltpu.SMEM(type_weight.shape, f32),
                pltpu.SMEM(crowd_cost.shape, f32),
                pltpu.SMEM(exit_drain.shape, f32),
                pltpu.SMEM(exit_type.shape, jnp.int32),
                pltpu.SMEM(landing_fields.shape, jnp.int32),
                dma((tiles,)),
                dma((tiles,)),
                dma((7,)),
                dma((tiles,)),
                dma((tiles,)),
                dma((strips,)),
                dma((strips,)),
                dma((floors,)),
                dma((floors,)),
                dma((floors,)),
                dma((floors,)),
                dma((n, strips)),
                dma((n, strips)),
                dma((n, strips)),
                dma((n, strips)),
                dma((n, 2)),
                dma((n, 2)),
                dma((n, 2)),
                dma((n, 2)),
                dma((n,)),
                dma((n,)),
            ],
            compiler_params=pltpu.CompilerParams(
                collective_id=0, has_side_effects=True, vmem_limit_bytes=64 * 1024 * 1024
            ),
        )(density, value_field, row_kernel, column_kernel, type_weight, crowd_cost, exit_drain, exit_type, landing_fields)
        return pl.pallas_call(
            finish,
            out_shape=(
                jax.ShapeDtypeStruct(density.shape, f32),
                jax.ShapeDtypeStruct(value_field.shape, f32),
            ),
            in_specs=[any_spec] * 2,
            out_specs=(any_spec, any_spec),
            scratch_shapes=[pltpu.VMEM((2, types, rows, width), f32), dma((2, types)), dma((2, types))],
            compiler_params=pltpu.CompilerParams(vmem_limit_bytes=64 * 1024 * 1024),
        )(*new)

    placed = (
        P("floor", None, "strip", None),
        P("floor", None, "strip", None),
        P("strip", None),
        P(),
        P(),
        P(),
        P(),
        P("floor", "strip"),
        P(None, "strip", None),
    )
    return jax.shard_map(
        local,
        mesh=mesh,
        in_specs=placed,
        out_specs=(P("floor", None, "strip", None), P("floor", None, "strip", None)),
        check_vma=False,
    )
```

```python
import functools

import jax
import jax.numpy as jnp
from jax import lax
from jax.experimental import pallas as pl
from jax.experimental.pallas import tpu as pltpu
from jax.sharding import PartitionSpec as P

SUBSTEPS = 4
TILES = 16
LANE = 128
TOP = 8

time_step = 0.2
viscosity = 1.0
exit_reward = 2.0
stair_rate = 0.5

MESH = pl.DeviceIdType.MESH


def kernel(
    strips, floors, landings, types, rows, width,
    dens_hbm, val_hbm, rk_hbm, ck_hbm, tw_hbm, cc_hbm, ed_hbm, et_hbm, lm_hbm,
    dens_out, val_out,
    m0, m1, u0, u1, ck, rk, crowd_send, crowd_recv, mix_send, mix_recv,
    hm_send, hm_recv, hu_send, hu_recv, out_send, out_recv,
    drain_fac, reward, keep_map, dst_map, rk_own,
    tw_ref, cc_ref, ed_ref, et_ref, lm_ref,
    load_m, load_u, load_sem, store_m, store_u, rk_ssem, rk_rsem, rf_ssem, rf_rsem, rm_ssem, rm_rsem,
    c_ssem, c_rsem, x_ssem, x_rsem, hm_ssem, hm_rsem, hu_ssem, hu_rsem, o_ssem, o_rsem,
):
    me = lax.axis_index("strip")
    floor = lax.axis_index("floor")
    tiles = width // LANE
    cw = width // strips
    per = cw // LANE
    groups = rows // 8
    dq = rk.shape[-1]
    half = rows // 2
    core = lax.rem(me, 2)
    inner = pl.ds(TOP, rows)
    M, U = (m0, m1), (u0, u1)

    barrier = pltpu.get_barrier_semaphore()
    for off in range(1, strips):
        pl.semaphore_signal(barrier, inc=1, device_id={"strip": lax.rem(me + off, strips)}, device_id_type=MESH)
    for off in range(1, floors):
        pl.semaphore_signal(barrier, inc=1, device_id={"floor": lax.rem(floor + off, floors)}, device_id_type=MESH)

    def field_copy(hbm, buf, sem, c):
        return pltpu.make_async_copy(hbm.at[0, :, :, pl.ds(c * LANE, LANE)], buf.at[:, c, inner, :], sem.at[c])

    for c in range(tiles):
        field_copy(dens_hbm, m0, load_m, c).start()
    my_piece = pl.ds(pl.multiple_of(floor * dq, LANE), dq)
    own_rk = pltpu.make_async_copy(rk_hbm.at[:, my_piece], rk_own, load_sem.at[0])
    own_rk.start()
    small = [
        pltpu.make_async_copy(src, dst, load_sem.at[1 + i])
        for i, (src, dst) in enumerate(
            ((tw_hbm, tw_ref), (cc_hbm, cc_ref), (ed_hbm, ed_ref), (et_hbm, et_ref), (lm_hbm, lm_ref))
        )
    ]
    for copy in small:
        copy.start()
    for c in range(tiles):
        field_copy(val_hbm, u0, load_u, c).start()
    load_ck = pltpu.make_async_copy(ck_hbm, ck, load_sem.at[6])

    pl.semaphore_wait(barrier, strips + floors - 2)

    def strip_copy(src, dst, ssem, rsem, off):
        return pltpu.make_async_remote_copy(
            src_ref=src, dst_ref=dst, send_sem=ssem.at[off], recv_sem=rsem.at[off],
            device_id={"strip": lax.rem(me + off, strips)}, device_id_type=MESH,
        )

    def spread(step):
        return (strips // 2 + (1 - 2 * (step % 2)) * ((step + 1) // 2)) % strips

    order = [spread(step) for step in range(strips - 1)]

    def to_all(src_of, dst_ref, ssem, rsem):
        for off in order:
            strip_copy(src_of(lax.rem(me + off, strips)), dst_ref.at[me], ssem, rsem, off).start()

    def from_all(src_of, dst_ref, ssem, rsem):
        for off in range(1, strips):
            src = lax.rem(me + strips - off, strips)
            strip_copy(src_of(lax.rem(me + off, strips)), dst_ref.at[src], ssem, rsem, off).wait()

    def rk_hop(off):
        return pltpu.make_async_remote_copy(
            src_ref=rk.at[floor, core], dst_ref=rk.at[floor, core], send_sem=rf_ssem.at[off], recv_sem=rf_rsem.at[off],
            device_id={"floor": lax.rem(floor + off, floors)}, device_id_type=MESH,
        )

    def rk_landed(off):
        came = lax.rem(floor + floors - off, floors)
        return pltpu.make_async_remote_copy(
            src_ref=rk.at[floor, core], dst_ref=rk.at[came, core], send_sem=rf_ssem.at[off], recv_sem=rf_rsem.at[off],
            device_id={"floor": lax.rem(floor + off, floors)}, device_id_type=MESH,
        )

    def rk_mate(f, side):
        return pltpu.make_async_remote_copy(
            src_ref=rk.at[f, core], dst_ref=rk.at[f, side], send_sem=rm_ssem.at[f], recv_sem=rm_rsem.at[f],
            device_id={"strip": me + 1 - 2 * core}, device_id_type=MESH,
        )

    def rk_share(off, slot):
        side = lax.rem(lax.rem(me + off, strips), 2)
        rows_for = rk_own.at[pl.ds(pl.multiple_of(side * half, half), half), :]
        return strip_copy(rows_for, slot(side), rk_ssem, rk_rsem, off)

    def rim_copy(send, recv, ssem, rsem, t, side):
        return pltpu.make_async_remote_copy(
            src_ref=send.at[t, side], dst_ref=recv.at[t, 1 - side],
            send_sem=ssem.at[t, side], recv_sem=rsem.at[t, 1 - side],
            device_id={"strip": me - 1 if side == 0 else me + 1}, device_id_type=MESH,
        )

    def send_rims(buf, send, recv, ssem, rsem, t):
        def pack(side):
            at = TOP if side == 0 else TOP + rows - 1
            for k in range(types):
                row = jnp.concatenate([buf[k, c, at:at + 1, :] for c in range(tiles)], axis=0)
                send[t, side, k] = row.astype(jnp.bfloat16)
            rim_copy(send, recv, ssem, rsem, t, side).start()

        pl.when(me > 0)(lambda: pack(0))
        pl.when(me < strips - 1)(lambda: pack(1))

    def take_rims(buf, send, recv, ssem, rsem, t):
        def own(side):
            at = TOP if side == 0 else TOP + rows - 1
            to = TOP - 1 if side == 0 else TOP + rows
            for k in range(types):
                for c in range(tiles):
                    buf[k, c, to:to + 1, :] = buf[k, c, at:at + 1, :]

        def got(side):
            rim_copy(send, recv, ssem, rsem, t, side).wait_send()
            pltpu.make_async_remote_copy(
                src_ref=send.at[t, side], dst_ref=recv.at[t, side],
                send_sem=ssem.at[t, side], recv_sem=rsem.at[t, side],
                device_id={"strip": me - 1 if side == 0 else me + 1}, device_id_type=MESH,
            ).wait_recv()
            to = TOP - 1 if side == 0 else TOP + rows
            for k in range(types):
                row = recv[t, side, k].astype(jnp.float32)
                for c in range(tiles):
                    buf[k, c, to:to + 1, :] = row[c:c + 1, :]

        pl.when(me > 0)(lambda: got(0))
        pl.when(me == 0)(lambda: own(0))
        pl.when(me < strips - 1)(lambda: got(1))
        pl.when(me == strips - 1)(lambda: own(1))

    def crowd_of(t, initial):
        buf = M[t % 2]

        @pl.loop(0, strips)
        def _(step):
            off = lax.rem(step + 1, strips)
            dst = lax.rem(me + off, strips)
            for q in range(per):
                c = dst * per + q
                total = None
                if not initial:
                    keep = keep_map[c]
                    ids = dst_map[c]
                    slot = jnp.maximum(ids, 0)
                    landed = ids >= 0
                for k in range(types):
                    v = buf[k, c, inner, :]
                    if not initial:
                        if landings == 8:
                            add = jnp.concatenate([
                                jnp.take_along_axis(out_recv[t - 1, k], slot[r:r + 8], axis=0, mode="promise_in_bounds")
                                for r in range(0, rows, 8)
                            ], axis=0)
                            add = jnp.where(landed, add, 0.0)
                        else:
                            add = jnp.zeros_like(v)
                            for l in range(landings):
                                add = jnp.where(ids == l, out_recv[t - 1, k, l:l + 1, :], add)
                        v = v * keep + add
                        buf[k, c, inner, :] = v
                    term = tw_ref[k] * v
                    total = term if total is None else total + term
                if t < SUBSTEPS:
                    crowd_send[t, dst, :, q * LANE:(q + 1) * LANE] = total.astype(jnp.bfloat16)
                else:
                    pltpu.make_async_copy(
                        buf.at[:, c, inner, :],
                        dens_out.at[0, :, :, pl.ds(pl.multiple_of(c * LANE, LANE), LANE)],
                        store_m.at[c],
                    ).start()
            if t < SUBSTEPS:
                @pl.when(off > 0)
                def _():
                    strip_copy(crowd_send.at[t, dst], crowd_recv.at[t, me], c_ssem.at[t], c_rsem.at[t], off).start()

        if t < SUBSTEPS:
            crowd_recv[t, me] = crowd_send[t, me]

    def mix(t):
        from_all(lambda d: crowd_send.at[t, d], crowd_recv.at[t], c_ssem.at[t], c_rsem.at[t])
        crowd = crowd_recv[t].reshape(strips * rows, cw)
        group = strips // 2
        far = (1 - lax.div(me, group)) * group
        for base in (far, group - far):
            weights = jnp.concatenate([
                jnp.concatenate([rk[f, h, pl.ds(base, group)].reshape(group * half, dq) for f in range(floors)], axis=1)
                for h in range(2)
            ], axis=0)
            mixed = jnp.dot(weights, crowd, preferred_element_type=jnp.float32).astype(jnp.bfloat16)
            for h in range(2):
                mix_send[t, pl.ds(base, group), h * half:(h + 1) * half, :] = (
                    mixed[h * group * half:(h + 1) * group * half].reshape(group, half, cw)
                )
            for i in range(group):
                off = lax.rem(base + lax.rem(me + i, group) - me + strips, strips)

                @pl.when(off > 0)
                def _():
                    strip_copy(mix_send.at[t, lax.rem(me + off, strips)], mix_recv.at[t, me], x_ssem.at[t], x_rsem.at[t], off).start()
        mix_recv[t, me] = mix_send[t, me]

    def add_potential(t):
        buf = U[(t + 1) % 2]
        from_all(lambda d: mix_send.at[t, d], mix_recv.at[t], x_ssem.at[t], x_rsem.at[t])
        step = 4 * LANE

        @pl.loop(0, width // step)
        def _(n):
            start = pl.multiple_of(n * step, step)
            acc = None
            for s in range(strips):
                d = jnp.dot(mix_recv[t, s], ck[s * cw:(s + 1) * cw, pl.ds(start, step)], preferred_element_type=jnp.float32)
                acc = d if acc is None else acc + d
            for q in range(4):
                c = 4 * n + q
                part = acc[:, q * LANE:(q + 1) * LANE]
                for k in range(types):
                    buf[k, c, inner, :] = buf[k, c, inner, :] + (time_step * cc_ref[k]) * part
                if t == SUBSTEPS - 1:
                    pltpu.make_async_copy(
                        buf.at[:, c, inner, :],
                        val_out.at[0, :, :, pl.ds(pl.multiple_of(c * LANE, LANE), LANE)],
                        store_u.at[c],
                    ).start()

    lane = lax.broadcasted_iota(jnp.int32, (8, LANE), 1)
    first, last = lane == 0, lane == LANE - 1

    def stencil(t, chunks):
        mb, ub, mo, uo = M[t % 2], U[t % 2], M[(t + 1) % 2], U[(t + 1) % 2]

        @pl.loop(0, types)
        def _(k):
            for r in chunks:
                lo = TOP + 8 * r
                here = slice(lo, lo + 8)
                m, u = mb[k, 0, here, :], ub[k, 0, here, :]
                m_from, u_from = m, u
                m_back, u_back = pltpu.roll(m, LANE - 1, 1), pltpu.roll(u, LANE - 1, 1)
                for c in range(tiles):
                    if c < tiles - 1:
                        m_next, u_next = mb[k, c + 1, here, :], ub[k, c + 1, here, :]
                        m_next_back, u_next_back = pltpu.roll(m_next, LANE - 1, 1), pltpu.roll(u_next, LANE - 1, 1)
                    else:
                        m_next, u_next, m_next_back, u_next_back = m, u, m, u
                    mr, ur = jnp.where(last, m_next_back, m_back), jnp.where(last, u_next_back, u_back)
                    m_on, u_on = pltpu.roll(m, 1, 1), pltpu.roll(u, 1, 1)
                    ml, ul = jnp.where(first, m_from, m_on), jnp.where(first, u_from, u_on)
                    mu, md = mb[k, c, lo - 1:lo + 7, :], mb[k, c, lo + 1:lo + 9, :]
                    uu, ud = ub[k, c, lo - 1:lo + 7, :], ub[k, c, lo + 1:lo + 9, :]
                    low = u - 2.0 * viscosity
                    flux = None
                    rise = None
                    for mn, un in ((mu, uu), (md, ud), (ml, ul), (mr, ur)):
                        p = un - low
                        flux = mn * p if flux is None else flux + mn * p
                        rise = p if rise is None else rise + p
                    gr = ud - uu
                    gc = ur - ul
                    stay = (1.0 - 8.0 * viscosity * time_step) / (0.5 * time_step)
                    mo[k, c, here, :] = (flux + m * (rise + stay)) * drain_fac[k, c]
                    uo[k, c, here, :] = (u - reward[k, c]) + (time_step * viscosity) * (
                        rise - (0.125 / viscosity) * (gr * gr + gc * gc)
                    )
                    m, u, m_back, u_back, m_from, u_from = m_next, u_next, m_next_back, u_next_back, m_on, u_on

    def out_copy(t):
        return pltpu.make_async_remote_copy(
            src_ref=out_send.at[t], dst_ref=out_recv.at[t],
            send_sem=o_ssem.at[t], recv_sem=o_rsem.at[t],
            device_id={"floor": floor - 1}, device_id_type=MESH,
        )

    def stairs(t):
        buf = M[(t + 1) % 2]
        for l in range(landings):
            face = buf[:, lm_ref[floor, 0, l], pl.ds(TOP + lm_ref[floor, 1, l], 1), :]
            out_send[t, :, l:l + 1, :] = stair_rate * face

        @pl.when(floor > 0)
        def _():
            out_copy(t).start()

    def stairs_in(t):
        @pl.when(floor > 0)
        def _():
            out_copy(t).wait_send()

        @pl.when(floor < floors - 1)
        def _():
            out_copy(t).wait_recv()

        @pl.when(floor == floors - 1)
        def _():
            out_recv[t] = jnp.zeros_like(out_recv[t])

    hm = (hm_send, hm_recv, hm_ssem, hm_rsem)
    hu = (hu_send, hu_recv, hu_ssem, hu_rsem)

    own_rk.wait()
    for off in order:
        rk_share(off, lambda side: rk.at[floor, side, me]).start()
    for copy in small:
        copy.wait()
    for c in range(tiles):
        field_copy(dens_hbm, m0, load_m, c).wait()
    crowd_of(0, True)
    load_ck.start()
    for off in range(1, strips):
        src = lax.rem(me + strips - off, strips)
        rk_share(off, lambda side: rk.at[floor, core, src]).wait()
    rk[floor, core, me] = rk_own[pl.ds(pl.multiple_of(core * half, half), half), :]
    for off in range(1, floors):
        rk_hop(off).start()
    rk_mate(floor, core).start()

    send_rims(m0, *hm, 0)
    for c in range(tiles):
        field_copy(val_hbm, u0, load_u, c).wait()
    send_rims(u0, *hu, 0)

    above = jnp.minimum(floor + 1, floors - 1)
    tile_cols = width // TILES
    for tile in range(TILES):
        kind = et_ref[0, tile]
        for k in range(types):
            hit = jnp.where(kind == k, 1.0, 0.0).astype(jnp.float32)
            for c in range(tile * tile_cols // LANE, (tile + 1) * tile_cols // LANE):
                drain_fac[k, c] = jnp.full((8, LANE), (0.5 * time_step) * (1.0 - ed_ref[k] * hit), jnp.float32)
                reward[k, c] = jnp.full((8, LANE), time_step * exit_reward * hit + 8.0 * viscosity * viscosity * time_step, jnp.float32)

    stencil(0, range(1, groups - 1))

    for off in range(1, floors):
        rk_landed(off).wait()
        rk_mate(lax.rem(floor + floors - off, floors), core).start()

    row_at = lax.broadcasted_iota(jnp.int32, (rows, LANE), 0)

    @pl.loop(0, TILES)
    def _(tile):
        keep = jnp.ones((rows, LANE), jnp.float32)
        ids = jnp.full((rows, LANE), -1, jnp.int32)
        for l in range(landings):
            src_row = jnp.where(lm_ref[floor, 0, l] == tile, lm_ref[floor, 1, l], -1)
            dst_row = jnp.where(lm_ref[above, 2, l] == tile, lm_ref[above, 3, l], -1)
            keep = jnp.where(row_at == src_row, 1.0 - stair_rate, keep)
            ids = jnp.where(row_at == dst_row, l, ids)
        keep_map[tile] = keep
        dst_map[tile] = ids

    for t in range(SUBSTEPS):
        if t > 0:
            if t == 1:
                load_ck.wait()
            add_potential(t - 1)
            send_rims(U[t % 2], *hu, t)
            stencil(t, range(1, groups - 1))
        if t == 0:
            for f in range(floors):
                rk_mate(f, 1 - core).wait()
        mix(t)
        take_rims(M[t % 2], *hm, t)
        take_rims(U[t % 2], *hu, t)
        stencil(t, (0, groups - 1))
        stairs(t)
        stairs_in(t)
        crowd_of(t + 1, False)
        if t + 1 < SUBSTEPS:
            send_rims(M[(t + 1) % 2], *hm, t + 1)
    add_potential(SUBSTEPS - 1)
    end = SUBSTEPS % 2
    for c in range(tiles):
        here = pl.ds(c * LANE, LANE)
        pltpu.make_async_copy(M[end].at[:, c, inner, :], dens_out.at[0, :, :, here], store_m.at[c]).wait()
        pltpu.make_async_copy(U[end].at[:, c, inner, :], val_out.at[0, :, :, here], store_u.at[c]).wait()


def finish(m_in, u_in, m_out, u_out, held, in_sem, out_sem):
    into, out = [], []
    for i, (src, dst) in enumerate(((m_in, m_out), (u_in, u_out))):
        for k in range(src.shape[1]):
            into.append(pltpu.make_async_copy(src.at[0, k], held.at[i, k], in_sem.at[i, k]))
            out.append(pltpu.make_async_copy(held.at[i, k], dst.at[0, k], out_sem.at[i, k]))
    for copy in into:
        copy.start()
    for came, leaves in zip(into, out):
        came.wait()
        leaves.start()
    for copy in out:
        copy.wait()


def solution(mesh):
    strips = mesh.shape["strip"]
    floors = mesh.shape["floor"]

    def local(density, value_field, row_kernel, column_kernel, type_weight, crowd_cost, exit_drain, exit_type, landing_map):
        _, types, rows, width = density.shape
        landings = landing_map.shape[1]
        depth = row_kernel.shape[1]
        cw = width // strips
        tiles = width // LANE
        n = SUBSTEPS
        any_spec = pl.BlockSpec(memory_space=pltpu.HBM)
        f32, bf16 = jnp.float32, jnp.bfloat16
        dma = pltpu.SemaphoreType.DMA
        field = pltpu.VMEM((types, tiles, rows + 2 * TOP, LANE), f32)
        landing_fields = jnp.transpose(landing_map, (0, 2, 1))
        new = pl.pallas_call(
            functools.partial(kernel, strips, floors, landings, types, rows, width),
            out_shape=(
                jax.ShapeDtypeStruct(density.shape, f32),
                jax.ShapeDtypeStruct(value_field.shape, f32),
            ),
            in_specs=[any_spec] * 9,
            out_specs=(any_spec, any_spec),
            scratch_shapes=[
                field,
                field,
                field,
                field,
                pltpu.VMEM(column_kernel.shape, bf16),
                pltpu.VMEM((floors, 2, strips, rows // 2, depth // floors), bf16),
                pltpu.VMEM((n, strips, rows, cw), bf16),
                pltpu.VMEM((n, strips, rows, cw), bf16),
                pltpu.VMEM((n, strips, rows, cw), bf16),
                pltpu.VMEM((n, strips, rows, cw), bf16),
                pltpu.VMEM((n, 2, types, tiles, LANE), bf16),
                pltpu.VMEM((n, 2, types, tiles, LANE), bf16),
                pltpu.VMEM((n, 2, types, tiles, LANE), bf16),
                pltpu.VMEM((n, 2, types, tiles, LANE), bf16),
                pltpu.VMEM((n, types, landings, LANE), f32),
                pltpu.VMEM((n, types, landings, LANE), f32),
                pltpu.VMEM((types, tiles, 8, LANE), f32),
                pltpu.VMEM((types, tiles, 8, LANE), f32),
                pltpu.VMEM((TILES, rows, LANE), f32),
                pltpu.VMEM((TILES, rows, LANE), jnp.int32),
                pltpu.VMEM((rows, depth // floors), bf16),
                pltpu.SMEM(type_weight.shape, f32),
                pltpu.SMEM(crowd_cost.shape, f32),
                pltpu.SMEM(exit_drain.shape, f32),
                pltpu.SMEM(exit_type.shape, jnp.int32),
                pltpu.SMEM(landing_fields.shape, jnp.int32),
                dma((tiles,)),
                dma((tiles,)),
                dma((7,)),
                dma((tiles,)),
                dma((tiles,)),
                dma((strips,)),
                dma((strips,)),
                dma((floors,)),
                dma((floors,)),
                dma((floors,)),
                dma((floors,)),
                dma((n, strips)),
                dma((n, strips)),
                dma((n, strips)),
                dma((n, strips)),
                dma((n, 2)),
                dma((n, 2)),
                dma((n, 2)),
                dma((n, 2)),
                dma((n,)),
                dma((n,)),
            ],
            compiler_params=pltpu.CompilerParams(
                collective_id=0, has_side_effects=True, vmem_limit_bytes=64 * 1024 * 1024
            ),
        )(density, value_field, row_kernel, column_kernel, type_weight, crowd_cost, exit_drain, exit_type, landing_fields)
        return pl.pallas_call(
            finish,
            out_shape=(
                jax.ShapeDtypeStruct(density.shape, f32),
                jax.ShapeDtypeStruct(value_field.shape, f32),
            ),
            in_specs=[any_spec] * 2,
            out_specs=(any_spec, any_spec),
            scratch_shapes=[pltpu.VMEM((2, types, rows, width), f32), dma((2, types)), dma((2, types))],
            compiler_params=pltpu.CompilerParams(vmem_limit_bytes=64 * 1024 * 1024),
        )(*new)

    placed = (
        P("floor", None, "strip", None),
        P("floor", None, "strip", None),
        P("strip", None),
        P(),
        P(),
        P(),
        P(),
        P("floor", "strip"),
        P(None, "strip", None),
    )
    return jax.shard_map(
        local,
        mesh=mesh,
        in_specs=placed,
        out_specs=(P("floor", None, "strip", None), P("floor", None, "strip", None)),
        check_vma=False,
    )
```

```python
import functools

import jax
import jax.numpy as jnp
from jax import lax
from jax.experimental import pallas as pl
from jax.experimental.pallas import tpu as pltpu
from jax.sharding import PartitionSpec as P

SUBSTEPS = 4
TILES = 16
LANE = 128
TOP = 8

time_step = 0.2
viscosity = 1.0
exit_reward = 2.0
stair_rate = 0.5

MESH = pl.DeviceIdType.MESH


def kernel(
    strips, floors, landings, types, rows, width,
    dens_hbm, val_hbm, rk_hbm, ck_hbm, tw_hbm, cc_hbm, ed_hbm, et_hbm, lm_hbm,
    dens_out, val_out,
    m0, m1, u0, u1, ck, rk, crowd_send, crowd_recv, mix_send, mix_recv,
    hm_send, hm_recv, hu_send, hu_recv, out_send, out_recv,
    drain_fac, reward, keep_map, dst_map, rk_own,
    tw_ref, cc_ref, ed_ref, et_ref, lm_ref,
    load_m, load_u, load_sem, store_m, store_u, rk_ssem, rk_rsem, rf_ssem, rf_rsem, rm_ssem, rm_rsem,
    c_ssem, c_rsem, x_ssem, x_rsem, hm_ssem, hm_rsem, hu_ssem, hu_rsem, o_ssem, o_rsem,
):
    me = lax.axis_index("strip")
    floor = lax.axis_index("floor")
    tiles = width // LANE
    cw = width // strips
    per = cw // LANE
    groups = rows // 8
    dq = rk.shape[-1]
    half = rows // 2
    core = lax.rem(me, 2)
    inner = pl.ds(TOP, rows)
    M, U = (m0, m1), (u0, u1)

    barrier = pltpu.get_barrier_semaphore()
    for off in range(1, strips):
        pl.semaphore_signal(barrier, inc=1, device_id={"strip": lax.rem(me + off, strips)}, device_id_type=MESH)
    for off in range(1, floors):
        pl.semaphore_signal(barrier, inc=1, device_id={"floor": lax.rem(floor + off, floors)}, device_id_type=MESH)

    def field_copy(hbm, buf, sem, c):
        return pltpu.make_async_copy(hbm.at[0, :, :, pl.ds(c * LANE, LANE)], buf.at[:, c, inner, :], sem.at[c])

    for c in range(tiles):
        field_copy(dens_hbm, m0, load_m, c).start()
    my_piece = pl.ds(pl.multiple_of(floor * dq, LANE), dq)
    own_rk = pltpu.make_async_copy(rk_hbm.at[:, my_piece], rk_own, load_sem.at[0])
    own_rk.start()
    small = [
        pltpu.make_async_copy(src, dst, load_sem.at[1 + i])
        for i, (src, dst) in enumerate(
            ((tw_hbm, tw_ref), (cc_hbm, cc_ref), (ed_hbm, ed_ref), (et_hbm, et_ref), (lm_hbm, lm_ref))
        )
    ]
    for copy in small:
        copy.start()
    for c in range(tiles):
        field_copy(val_hbm, u0, load_u, c).start()
    load_ck = pltpu.make_async_copy(ck_hbm, ck, load_sem.at[6])

    pl.semaphore_wait(barrier, strips + floors - 2)

    def strip_copy(src, dst, ssem, rsem, off):
        return pltpu.make_async_remote_copy(
            src_ref=src, dst_ref=dst, send_sem=ssem.at[off], recv_sem=rsem.at[off],
            device_id={"strip": lax.rem(me + off, strips)}, device_id_type=MESH,
        )

    def spread(step):
        return (strips // 2 + (1 - 2 * (step % 2)) * ((step + 1) // 2)) % strips

    order = [spread(step) for step in range(strips - 1)]

    def to_all(src_of, dst_ref, ssem, rsem):
        for off in order:
            strip_copy(src_of(lax.rem(me + off, strips)), dst_ref.at[me], ssem, rsem, off).start()

    def from_all(src_of, dst_ref, ssem, rsem):
        for off in range(1, strips):
            src = lax.rem(me + strips - off, strips)
            strip_copy(src_of(lax.rem(me + off, strips)), dst_ref.at[src], ssem, rsem, off).wait()

    def rk_hop(off):
        return pltpu.make_async_remote_copy(
            src_ref=rk.at[floor, core], dst_ref=rk.at[floor, core], send_sem=rf_ssem.at[off], recv_sem=rf_rsem.at[off],
            device_id={"floor": lax.rem(floor + off, floors)}, device_id_type=MESH,
        )

    def rk_landed(off):
        came = lax.rem(floor + floors - off, floors)
        return pltpu.make_async_remote_copy(
            src_ref=rk.at[floor, core], dst_ref=rk.at[came, core], send_sem=rf_ssem.at[off], recv_sem=rf_rsem.at[off],
            device_id={"floor": lax.rem(floor + off, floors)}, device_id_type=MESH,
        )

    def rk_mate(f, side):
        return pltpu.make_async_remote_copy(
            src_ref=rk.at[f, core], dst_ref=rk.at[f, side], send_sem=rm_ssem.at[f], recv_sem=rm_rsem.at[f],
            device_id={"strip": me + 1 - 2 * core}, device_id_type=MESH,
        )

    def rk_share(off, slot):
        side = lax.rem(lax.rem(me + off, strips), 2)
        rows_for = rk_own.at[pl.ds(pl.multiple_of(side * half, half), half), :]
        return strip_copy(rows_for, slot(side), rk_ssem, rk_rsem, off)

    def rim_copy(send, recv, ssem, rsem, t, side):
        return pltpu.make_async_remote_copy(
            src_ref=send.at[t, side], dst_ref=recv.at[t, 1 - side],
            send_sem=ssem.at[t, side], recv_sem=rsem.at[t, 1 - side],
            device_id={"strip": me - 1 if side == 0 else me + 1}, device_id_type=MESH,
        )

    def send_rims(buf, send, recv, ssem, rsem, t):
        def pack(side):
            at = TOP if side == 0 else TOP + rows - 1
            for k in range(types):
                row = jnp.concatenate([buf[k, c, at:at + 1, :] for c in range(tiles)], axis=0)
                send[t, side, k] = row.astype(jnp.bfloat16)
            rim_copy(send, recv, ssem, rsem, t, side).start()

        pl.when(me > 0)(lambda: pack(0))
        pl.when(me < strips - 1)(lambda: pack(1))

    def take_rims(buf, send, recv, ssem, rsem, t):
        def own(side):
            at = TOP if side == 0 else TOP + rows - 1
            to = TOP - 1 if side == 0 else TOP + rows
            for k in range(types):
                for c in range(tiles):
                    buf[k, c, to:to + 1, :] = buf[k, c, at:at + 1, :]

        def got(side):
            rim_copy(send, recv, ssem, rsem, t, side).wait_send()
            pltpu.make_async_remote_copy(
                src_ref=send.at[t, side], dst_ref=recv.at[t, side],
                send_sem=ssem.at[t, side], recv_sem=rsem.at[t, side],
                device_id={"strip": me - 1 if side == 0 else me + 1}, device_id_type=MESH,
            ).wait_recv()
            to = TOP - 1 if side == 0 else TOP + rows
            for k in range(types):
                row = recv[t, side, k].astype(jnp.float32)
                for c in range(tiles):
                    buf[k, c, to:to + 1, :] = row[c:c + 1, :]

        pl.when(me > 0)(lambda: got(0))
        pl.when(me == 0)(lambda: own(0))
        pl.when(me < strips - 1)(lambda: got(1))
        pl.when(me == strips - 1)(lambda: own(1))

    def crowd_of(t, initial):
        buf = M[t % 2]

        @pl.loop(0, strips)
        def _(step):
            off = lax.rem(step + 1, strips)
            dst = lax.rem(me + off, strips)
            for q in range(per):
                c = dst * per + q
                total = None
                if not initial:
                    keep = keep_map[c]
                    ids = dst_map[c]
                    slot = jnp.maximum(ids, 0)
                    landed = ids >= 0
                for k in range(types):
                    v = buf[k, c, inner, :]
                    if not initial:
                        if landings == 8:
                            add = jnp.concatenate([
                                jnp.take_along_axis(out_recv[t - 1, k], slot[r:r + 8], axis=0, mode="promise_in_bounds")
                                for r in range(0, rows, 8)
                            ], axis=0)
                            add = jnp.where(landed, add, 0.0)
                        else:
                            add = jnp.zeros_like(v)
                            for l in range(landings):
                                add = jnp.where(ids == l, out_recv[t - 1, k, l:l + 1, :], add)
                        v = v * keep + add
                        buf[k, c, inner, :] = v
                    term = tw_ref[k] * v
                    total = term if total is None else total + term
                if t < SUBSTEPS:
                    crowd_send[t, dst, :, q * LANE:(q + 1) * LANE] = total.astype(jnp.bfloat16)
                else:
                    pltpu.make_async_copy(
                        buf.at[:, c, inner, :],
                        dens_out.at[0, :, :, pl.ds(pl.multiple_of(c * LANE, LANE), LANE)],
                        store_m.at[c],
                    ).start()
            if t < SUBSTEPS:
                @pl.when(off > 0)
                def _():
                    strip_copy(crowd_send.at[t, dst], crowd_recv.at[t, me], c_ssem.at[t], c_rsem.at[t], off).start()

        if t < SUBSTEPS:
            crowd_recv[t, me] = crowd_send[t, me]

    def mix(t):
        from_all(lambda d: crowd_send.at[t, d], crowd_recv.at[t], c_ssem.at[t], c_rsem.at[t])
        crowd = crowd_recv[t].reshape(strips * rows, cw)
        group = strips // 2
        far = (1 - lax.div(me, group)) * group
        for base in (far, group - far):
            weights = jnp.concatenate([
                jnp.concatenate([rk[f, h, pl.ds(base, group)].reshape(group * half, dq) for f in range(floors)], axis=1)
                for h in range(2)
            ], axis=0)
            mixed = jnp.dot(weights, crowd, preferred_element_type=jnp.float32).astype(jnp.bfloat16)
            for h in range(2):
                mix_send[t, pl.ds(base, group), h * half:(h + 1) * half, :] = (
                    mixed[h * group * half:(h + 1) * group * half].reshape(group, half, cw)
                )
            for i in range(group):
                off = lax.rem(base + lax.rem(me + i, group) - me + strips, strips)

                @pl.when(off > 0)
                def _():
                    strip_copy(mix_send.at[t, lax.rem(me + off, strips)], mix_recv.at[t, me], x_ssem.at[t], x_rsem.at[t], off).start()
        mix_recv[t, me] = mix_send[t, me]

    def add_potential(t):
        buf = U[(t + 1) % 2]
        from_all(lambda d: mix_send.at[t, d], mix_recv.at[t], x_ssem.at[t], x_rsem.at[t])
        step = 8 * LANE

        @pl.loop(0, width // step)
        def _(n):
            start = pl.multiple_of(n * step, step)
            acc = None
            for s in range(strips):
                d = jnp.dot(mix_recv[t, s], ck[s * cw:(s + 1) * cw, pl.ds(start, step)], preferred_element_type=jnp.float32)
                acc = d if acc is None else acc + d
            for q in range(8):
                c = 8 * n + q
                part = acc[:, q * LANE:(q + 1) * LANE]
                for k in range(types):
                    buf[k, c, inner, :] = buf[k, c, inner, :] + (time_step * cc_ref[k]) * part
                if t == SUBSTEPS - 1:
                    pltpu.make_async_copy(
                        buf.at[:, c, inner, :],
                        val_out.at[0, :, :, pl.ds(pl.multiple_of(c * LANE, LANE), LANE)],
                        store_u.at[c],
                    ).start()

    lane = lax.broadcasted_iota(jnp.int32, (8, LANE), 1)
    first, last = lane == 0, lane == LANE - 1

    def stencil(t, chunks):
        mb, ub, mo, uo = M[t % 2], U[t % 2], M[(t + 1) % 2], U[(t + 1) % 2]

        @pl.loop(0, types)
        def _(k):
            for r in chunks:
                lo = TOP + 8 * r
                here = slice(lo, lo + 8)
                m, u = mb[k, 0, here, :], ub[k, 0, here, :]
                m_from, u_from = m, u
                m_back, u_back = pltpu.roll(m, LANE - 1, 1), pltpu.roll(u, LANE - 1, 1)
                for c in range(tiles):
                    if c < tiles - 1:
                        m_next, u_next = mb[k, c + 1, here, :], ub[k, c + 1, here, :]
                        m_next_back, u_next_back = pltpu.roll(m_next, LANE - 1, 1), pltpu.roll(u_next, LANE - 1, 1)
                    else:
                        m_next, u_next, m_next_back, u_next_back = m, u, m, u
                    mr, ur = jnp.where(last, m_next_back, m_back), jnp.where(last, u_next_back, u_back)
                    m_on, u_on = pltpu.roll(m, 1, 1), pltpu.roll(u, 1, 1)
                    ml, ul = jnp.where(first, m_from, m_on), jnp.where(first, u_from, u_on)
                    mu, md = mb[k, c, lo - 1:lo + 7, :], mb[k, c, lo + 1:lo + 9, :]
                    uu, ud = ub[k, c, lo - 1:lo + 7, :], ub[k, c, lo + 1:lo + 9, :]
                    low = u - 2.0 * viscosity
                    flux = None
                    rise = None
                    for mn, un in ((mu, uu), (md, ud), (ml, ul), (mr, ur)):
                        p = un - low
                        flux = mn * p if flux is None else flux + mn * p
                        rise = p if rise is None else rise + p
                    gr = ud - uu
                    gc = ur - ul
                    stay = (1.0 - 8.0 * viscosity * time_step) / (0.5 * time_step)
                    mo[k, c, here, :] = (flux + m * (rise + stay)) * drain_fac[k, c]
                    uo[k, c, here, :] = (u - reward[k, c]) + (time_step * viscosity) * (
                        rise - (0.125 / viscosity) * (gr * gr + gc * gc)
                    )
                    m, u, m_back, u_back, m_from, u_from = m_next, u_next, m_next_back, u_next_back, m_on, u_on

    def out_copy(t):
        return pltpu.make_async_remote_copy(
            src_ref=out_send.at[t], dst_ref=out_recv.at[t],
            send_sem=o_ssem.at[t], recv_sem=o_rsem.at[t],
            device_id={"floor": floor - 1}, device_id_type=MESH,
        )

    def stairs(t):
        buf = M[(t + 1) % 2]
        for l in range(landings):
            face = buf[:, lm_ref[floor, 0, l], pl.ds(TOP + lm_ref[floor, 1, l], 1), :]
            out_send[t, :, l:l + 1, :] = stair_rate * face

        @pl.when(floor > 0)
        def _():
            out_copy(t).start()

    def stairs_in(t):
        @pl.when(floor > 0)
        def _():
            out_copy(t).wait_send()

        @pl.when(floor < floors - 1)
        def _():
            out_copy(t).wait_recv()

        @pl.when(floor == floors - 1)
        def _():
            out_recv[t] = jnp.zeros_like(out_recv[t])

    hm = (hm_send, hm_recv, hm_ssem, hm_rsem)
    hu = (hu_send, hu_recv, hu_ssem, hu_rsem)

    own_rk.wait()
    for off in order:
        rk_share(off, lambda side: rk.at[floor, side, me]).start()
    for copy in small:
        copy.wait()
    for c in range(tiles):
        field_copy(dens_hbm, m0, load_m, c).wait()
    crowd_of(0, True)
    load_ck.start()
    for off in range(1, strips):
        src = lax.rem(me + strips - off, strips)
        rk_share(off, lambda side: rk.at[floor, core, src]).wait()
    rk[floor, core, me] = rk_own[pl.ds(pl.multiple_of(core * half, half), half), :]
    for off in range(1, floors):
        rk_hop(off).start()
    rk_mate(floor, core).start()

    send_rims(m0, *hm, 0)
    for c in range(tiles):
        field_copy(val_hbm, u0, load_u, c).wait()
    send_rims(u0, *hu, 0)

    above = jnp.minimum(floor + 1, floors - 1)
    tile_cols = width // TILES
    for tile in range(TILES):
        kind = et_ref[0, tile]
        for k in range(types):
            hit = jnp.where(kind == k, 1.0, 0.0).astype(jnp.float32)
            for c in range(tile * tile_cols // LANE, (tile + 1) * tile_cols // LANE):
                drain_fac[k, c] = jnp.full((8, LANE), (0.5 * time_step) * (1.0 - ed_ref[k] * hit), jnp.float32)
                reward[k, c] = jnp.full((8, LANE), time_step * exit_reward * hit + 8.0 * viscosity * viscosity * time_step, jnp.float32)

    stencil(0, range(1, groups - 1))

    for off in range(1, floors):
        rk_landed(off).wait()
        rk_mate(lax.rem(floor + floors - off, floors), core).start()

    row_at = lax.broadcasted_iota(jnp.int32, (rows, LANE), 0)

    @pl.loop(0, TILES)
    def _(tile):
        keep = jnp.ones((rows, LANE), jnp.float32)
        ids = jnp.full((rows, LANE), -1, jnp.int32)
        for l in range(landings):
            src_row = jnp.where(lm_ref[floor, 0, l] == tile, lm_ref[floor, 1, l], -1)
            dst_row = jnp.where(lm_ref[above, 2, l] == tile, lm_ref[above, 3, l], -1)
            keep = jnp.where(row_at == src_row, 1.0 - stair_rate, keep)
            ids = jnp.where(row_at == dst_row, l, ids)
        keep_map[tile] = keep
        dst_map[tile] = ids

    for t in range(SUBSTEPS):
        if t > 0:
            if t == 1:
                load_ck.wait()
            add_potential(t - 1)
            send_rims(U[t % 2], *hu, t)
            stencil(t, range(1, groups - 1))
        if t == 0:
            for f in range(floors):
                rk_mate(f, 1 - core).wait()
        mix(t)
        take_rims(M[t % 2], *hm, t)
        take_rims(U[t % 2], *hu, t)
        stencil(t, (0, groups - 1))
        stairs(t)
        stairs_in(t)
        crowd_of(t + 1, False)
        if t + 1 < SUBSTEPS:
            send_rims(M[(t + 1) % 2], *hm, t + 1)
    add_potential(SUBSTEPS - 1)
    end = SUBSTEPS % 2
    for c in range(tiles):
        here = pl.ds(c * LANE, LANE)
        pltpu.make_async_copy(M[end].at[:, c, inner, :], dens_out.at[0, :, :, here], store_m.at[c]).wait()
        pltpu.make_async_copy(U[end].at[:, c, inner, :], val_out.at[0, :, :, here], store_u.at[c]).wait()


def finish(m_in, u_in, m_out, u_out, held, in_sem, out_sem):
    into, out = [], []
    for i, (src, dst) in enumerate(((m_in, m_out), (u_in, u_out))):
        for k in range(src.shape[1]):
            into.append(pltpu.make_async_copy(src.at[0, k], held.at[i, k], in_sem.at[i, k]))
            out.append(pltpu.make_async_copy(held.at[i, k], dst.at[0, k], out_sem.at[i, k]))
    for copy in into:
        copy.start()
    for came, leaves in zip(into, out):
        came.wait()
        leaves.start()
    for copy in out:
        copy.wait()


def solution(mesh):
    strips = mesh.shape["strip"]
    floors = mesh.shape["floor"]

    def local(density, value_field, row_kernel, column_kernel, type_weight, crowd_cost, exit_drain, exit_type, landing_map):
        _, types, rows, width = density.shape
        landings = landing_map.shape[1]
        depth = row_kernel.shape[1]
        cw = width // strips
        tiles = width // LANE
        n = SUBSTEPS
        any_spec = pl.BlockSpec(memory_space=pltpu.HBM)
        f32, bf16 = jnp.float32, jnp.bfloat16
        dma = pltpu.SemaphoreType.DMA
        field = pltpu.VMEM((types, tiles, rows + 2 * TOP, LANE), f32)
        landing_fields = jnp.transpose(landing_map, (0, 2, 1))
        new = pl.pallas_call(
            functools.partial(kernel, strips, floors, landings, types, rows, width),
            out_shape=(
                jax.ShapeDtypeStruct(density.shape, f32),
                jax.ShapeDtypeStruct(value_field.shape, f32),
            ),
            in_specs=[any_spec] * 9,
            out_specs=(any_spec, any_spec),
            scratch_shapes=[
                field,
                field,
                field,
                field,
                pltpu.VMEM(column_kernel.shape, bf16),
                pltpu.VMEM((floors, 2, strips, rows // 2, depth // floors), bf16),
                pltpu.VMEM((n, strips, rows, cw), bf16),
                pltpu.VMEM((n, strips, rows, cw), bf16),
                pltpu.VMEM((n, strips, rows, cw), bf16),
                pltpu.VMEM((n, strips, rows, cw), bf16),
                pltpu.VMEM((n, 2, types, tiles, LANE), bf16),
                pltpu.VMEM((n, 2, types, tiles, LANE), bf16),
                pltpu.VMEM((n, 2, types, tiles, LANE), bf16),
                pltpu.VMEM((n, 2, types, tiles, LANE), bf16),
                pltpu.VMEM((n, types, landings, LANE), f32),
                pltpu.VMEM((n, types, landings, LANE), f32),
                pltpu.VMEM((types, tiles, 8, LANE), f32),
                pltpu.VMEM((types, tiles, 8, LANE), f32),
                pltpu.VMEM((TILES, rows, LANE), f32),
                pltpu.VMEM((TILES, rows, LANE), jnp.int32),
                pltpu.VMEM((rows, depth // floors), bf16),
                pltpu.SMEM(type_weight.shape, f32),
                pltpu.SMEM(crowd_cost.shape, f32),
                pltpu.SMEM(exit_drain.shape, f32),
                pltpu.SMEM(exit_type.shape, jnp.int32),
                pltpu.SMEM(landing_fields.shape, jnp.int32),
                dma((tiles,)),
                dma((tiles,)),
                dma((7,)),
                dma((tiles,)),
                dma((tiles,)),
                dma((strips,)),
                dma((strips,)),
                dma((floors,)),
                dma((floors,)),
                dma((floors,)),
                dma((floors,)),
                dma((n, strips)),
                dma((n, strips)),
                dma((n, strips)),
                dma((n, strips)),
                dma((n, 2)),
                dma((n, 2)),
                dma((n, 2)),
                dma((n, 2)),
                dma((n,)),
                dma((n,)),
            ],
            compiler_params=pltpu.CompilerParams(
                collective_id=0, has_side_effects=True, vmem_limit_bytes=64 * 1024 * 1024
            ),
        )(density, value_field, row_kernel, column_kernel, type_weight, crowd_cost, exit_drain, exit_type, landing_fields)
        return pl.pallas_call(
            finish,
            out_shape=(
                jax.ShapeDtypeStruct(density.shape, f32),
                jax.ShapeDtypeStruct(value_field.shape, f32),
            ),
            in_specs=[any_spec] * 2,
            out_specs=(any_spec, any_spec),
            scratch_shapes=[pltpu.VMEM((2, types, rows, width), f32), dma((2, types)), dma((2, types))],
            compiler_params=pltpu.CompilerParams(vmem_limit_bytes=64 * 1024 * 1024),
        )(*new)

    placed = (
        P("floor", None, "strip", None),
        P("floor", None, "strip", None),
        P("strip", None),
        P(),
        P(),
        P(),
        P(),
        P("floor", "strip"),
        P(None, "strip", None),
    )
    return jax.shard_map(
        local,
        mesh=mesh,
        in_specs=placed,
        out_specs=(P("floor", None, "strip", None), P("floor", None, "strip", None)),
        check_vma=False,
    )
```
